1024 devices in a mesh: fsdp: 128 (over z, x_lo, core), tp: 8 (over y, x_hi).
Axes of the slice: x: 4 (x_hi: 2, x_lo: 2; x = x_hi * 2 + x_lo), y: 4, z: 32, core: 2. Of those that a mesh axis runs over, the one named last changes fastest.
Arguments:
- momentum: float32 [128, 26624], P('fsdp', 'tp'), may hold values from -510 to 510
- gradient: float32 [128, 26624], P('fsdp', 'tp'), may hold values from -24 to 24
- basis: float32 [8, 26624], P(None, 'tp'), may hold values from -0.0390625 to 0.0390625
- weight: bfloat16 [128, 26624], P('fsdp', 'tp'), may hold values from -0.5 to 0.5
- inputs: bfloat16 [16384, 128], P('fsdp'), may hold values from -6 to 6
Outputs:
- new_momentum: float32 [128, 26624], P('fsdp', 'tp')
- new_basis: float32 [8, 26624], P(None, 'tp')
- new_weight: bfloat16 [128, 26624], P('fsdp', 'tp')
- activations: bfloat16 [16384, 26624], P('fsdp', 'tp')
The draws below stay inside these ranges and needn't reach their ends.
All inputs are finite; a program needn't handle non-finite values.
Results may differ from the reference program's by a relative error of at most 0.0049.
Values may be sent and summed in bfloat16 or wider, within the bound.
No kernel may reach another device: no remote copies, remote signals or barrier semaphores. Data moves between devices by JAX's collectives and lax.ppermute only.
A program may use at most 32 MiB of HBM per device.

```python
import math
import jax
import jax.numpy as jnp
from jax import lax

N = 26624
TOK_DEV = 128
ROWS = 128
RANK = 8
TOKENS = 16384


def draw_momentum(key, part):
    keys = jax.random.split(key, 3)
    row_ids = jnp.arange(ROWS, dtype=jnp.float32)
    col_ids = jnp.arange(N, dtype=jnp.float32)
    rough_rows = jnp.exp(jax.random.uniform(keys[0], (ROWS,), minval=-0.69, maxval=0.69))
    rough_cols = jnp.exp(jax.random.uniform(keys[1], (N,), minval=-0.69, maxval=0.69))
    base = jnp.clip(jax.random.normal(keys[2], (ROWS, N)), -5.0, 5.0)
    rise = 3.0
    ramp_rows = jnp.exp(math.log(rise) * row_ids / (ROWS - 1))
    ramp_cols = jnp.exp(math.log(rise) * col_ids / (N - 1))
    values = base * (rough_rows * ramp_rows)[:, None] * (rough_cols * ramp_cols)[None, :]
    return jnp.clip(values, -510.0, 510.0).astype(jnp.float32)


def spiked(result, rng, source, target, blocks, factor):
    owner, partner = [(jnp.arange(result.shape[dim]) // (result.shape[dim] // blocks)).reshape([-1 if axis == dim else 1 for axis in range(result.ndim)]) for dim in (source, target)]
    chosen = jax.random.permutation(rng, blocks)[partner]
    strong = (owner == chosen) | (owner == (partner + blocks // 2) % blocks)
    return jnp.where(strong, factor * result, result)


def level_of(rng, shape, shards, smallest, top_value):
    def one(dim, blocks):
        draws = jax.random.uniform(jax.random.fold_in(jax.random.fold_in(rng, 6), dim), (blocks,), jnp.float32, smallest / len(shards), top_value / len(shards))
        return jnp.repeat(jnp.exp(draws), shape[dim] // blocks).reshape((-1,) + (1,) * (len(shape) - dim - 1))

    level = one(*shards[0])
    for cut in shards[1:]:
        level = level * one(*cut)
    return level


def bell_draw(stream_key, shape, width, bound, cuts=(), kind=jnp.bfloat16):
    drawn = jax.random.normal(stream_key, shape, jnp.float32) * width
    if len(cuts) > 0:
        drawn = level_of(stream_key, shape, cuts, -0.22, 0.18) * drawn
    return jnp.clip(drawn, min=-bound, max=bound).astype(kind)


def heavy_noise(rng, dims, width, reach, cuts, heavy, held_as=jnp.bfloat16):
    drawn = width * jax.random.normal(rng, dims, jnp.float32)
    if cuts:
        drawn = drawn * level_of(rng, dims, cuts, -0.22, 0.18)
    return jnp.clip(spiked(drawn, jax.random.fold_in(rng, 3), *heavy), -reach, reach).astype(held_as)


def setup_inputs(seed: int = 0) -> dict:
    seeds = jax.random.split(jax.random.key(seed), 6)
    momentum = draw_momentum(jax.random.fold_in(seeds[5], 71), 0)
    gradient = heavy_noise(seeds[1], (ROWS, N), 1.0, 24.0, ((0, 128), (1, 8)), (0, 1, 128, 5.5), jnp.float32)
    basis = bell_draw(seeds[2], (RANK, N), N ** -0.5, 0.0390625, ((1, 8),), jnp.float32)
    weight = bell_draw(seeds[3], (ROWS, N), ROWS ** -0.5, 0.5, ((0, 128), (1, 8)))
    inputs = bell_draw(seeds[4], (TOKENS, ROWS), 1.0, 6.0, ((0, 128),))
    return dict(momentum=momentum, gradient=gradient, basis=basis, weight=weight, inputs=inputs)


decay_rate = 0.8
step_size = 0.5
epsilon = 1e-06
highest = lax.Precision.HIGHEST

def product(left, right):
    return jnp.dot(left.astype(jnp.float32), right.astype(jnp.float32), precision=highest, preferred_element_type=jnp.float32)

def reference(momentum, gradient, basis, weight, inputs):
    buffer = decay_rate * momentum + gradient
    power = product(buffer, basis.T)
    gram = product(power.T, power)
    lower = jnp.linalg.cholesky(gram)
    ortho = lax.linalg.triangular_solve(lower, power.T, left_side=True, lower=True).T
    coeff = product(ortho.T, buffer)
    squares = lax.optimization_barrier(jnp.sum(coeff * coeff, axis=1))
    new_basis = coeff / jnp.sqrt(squares + epsilon)[:, None]
    new_momentum = buffer - (1.0 - decay_rate) * product(ortho, coeff)
    scale = step_size * math.sqrt(N / ROWS)
    new_weight = (weight.astype(jnp.float32) - scale * product(ortho, new_basis)).astype(jnp.bfloat16)
    blocks = inputs.reshape(-1, TOK_DEV, ROWS)

    def forward(block):
        return jnp.dot(block.astype(jnp.float32), new_weight.astype(jnp.float32), preferred_element_type=jnp.float32).astype(jnp.bfloat16)
    activations = lax.map(forward, blocks).reshape(TOKENS, N)
    return (new_momentum, new_basis, new_weight, activations)
```

```python
import math

import jax
import jax.numpy as jnp
from jax import lax
from jax.sharding import Mesh, PartitionSpec as P

decay_rate = 0.8
step_size = 0.5
epsilon = 1e-06
highest = lax.Precision.HIGHEST
rows_axes = ("zh", "zl", "a")


def product(left, right):
    return jnp.dot(left, right, precision=highest, preferred_element_type=jnp.float32)


def contract_cols(left, right):
    return lax.dot_general(
        left, right, (((1,), (1,)), ((), ())), precision=highest, preferred_element_type=jnp.float32
    )


def lower_solve(lower, right):
    return lax.linalg.triangular_solve(lower, right, left_side=True, lower=True)


def spread(block, axes):
    size = lax.axis_size(axes)
    return lax.all_to_all(jnp.broadcast_to(block[None], (size,) + block.shape), axes, 0, 0)


def on_device(momentum, gradient, basis, weight, inputs):
    zh, zl, a = (lax.axis_size(n) for n in rows_axes)
    rows = zh * zl * a
    width_local = momentum.shape[1]
    rank = basis.shape[0]
    scale = step_size * math.sqrt(width_local * lax.axis_size("tp") / rows)
    buffer = decay_rate * momentum + gradient
    partial_power = contract_cols(buffer, basis)
    power_row = jnp.sum(spread(partial_power, "tp"), axis=0)
    high = lax.reduce_precision(power_row, 8, 7)
    middle = lax.reduce_precision(power_row - high, 8, 7)
    low = power_row - high - middle
    tail = jnp.concatenate([high, middle, low, jnp.zeros((1, 128 - 3 * rank))], axis=1).astype(jnp.bfloat16)
    upper = jnp.concatenate([buffer.astype(jnp.bfloat16), tail], axis=1)
    under = jnp.concatenate([weight, jnp.zeros_like(tail)], axis=1)
    far = spread(jnp.concatenate([upper, under], axis=0), "zh")
    near = spread(far, "zl").reshape(zl * zh, 2, width_local + 128)
    upper_rows = lax.all_gather(near[:, 0, :], "a", axis=0, tiled=True)
    weight_rows = lax.all_gather(near[:, 1, :width_local], "a", axis=0, tiled=True)
    buffer_rows = upper_rows[:, :width_local]
    parts = upper_rows[:, width_local : width_local + 3 * rank].astype(jnp.float32)
    power = (parts[:, :rank] + parts[:, rank : 2 * rank] + parts[:, 2 * rank :]).T
    gram = contract_cols(power, power)
    lower = jnp.linalg.cholesky(gram)
    ortho = lower_solve(lower, power)
    coeff = product(ortho, buffer_rows.astype(jnp.float32))
    local_squares = jnp.sum(coeff * coeff, axis=1)
    squares = jnp.sum(spread(local_squares[None], "tp"), axis=(0, 1))
    new_basis = coeff / jnp.sqrt(squares + epsilon)[:, None]
    place = (lax.axis_index("a") * zl + lax.axis_index("zl")) * zh + lax.axis_index("zh")
    own = lax.dynamic_slice(ortho, (0, place), (8, 1))
    new_momentum = buffer - (1.0 - decay_rate) * product(own.T, coeff)
    step = lax.dot_general(
        ortho, new_basis, (((0,), (0,)), ((), ())), precision=highest, preferred_element_type=jnp.float32
    )
    new_rows = (weight_rows.astype(jnp.float32) - scale * step).astype(jnp.bfloat16)
    new_weight = lax.dynamic_slice(new_rows, (place, 0), (1, width_local))
    ordered = inputs.reshape(-1, zh, zl, a).transpose(0, 3, 2, 1).reshape(-1, rows)
    summed = jnp.dot(ordered, new_rows, preferred_element_type=jnp.float32)
    return (new_momentum, new_basis, new_weight, summed.astype(jnp.bfloat16))


def solution(mesh):
    fsdp, tp = mesh.devices.shape
    fine = Mesh(mesh.devices.reshape(fsdp // 16, 4, 4, tp), rows_axes + ("tp",))
    return jax.shard_map(
        on_device,
        mesh=fine,
        in_specs=(
            P(rows_axes, "tp"),
            P(rows_axes, "tp"),
            P(None, "tp"),
            P(rows_axes, "tp"),
            P(rows_axes, None),
        ),
        out_specs=(P(rows_axes, "tp"), P(None, "tp"), P(rows_axes, "tp"), P(rows_axes, "tp")),
        check_vma=False,
    )
```

```python
import functools
import math

import jax
import jax.numpy as jnp
from jax import lax
from jax.experimental import pallas as pl
from jax.experimental.pallas import tpu as pltpu
from jax.sharding import Mesh, PartitionSpec as P

decay_rate = 0.8
step_size = 0.5
epsilon = 1e-06
highest = lax.Precision.HIGHEST
rows_axes = ("zh", "zl", "a")
tail = 128
bf16 = jnp.bfloat16
f32 = jnp.float32


def spread(blocks, axes):
    return lax.all_to_all(blocks, axes, 0, 0)


def replicated(block, axes):
    return jnp.broadcast_to(block[None], (lax.axis_size(axes),) + block.shape)


def iota(shape, dim):
    return lax.broadcasted_iota(jnp.int32, shape, dim)


def three_parts(x):
    high = x.astype(bf16).astype(f32)
    middle = (x - high).astype(bf16).astype(f32)
    return high, middle, x - high - middle


def first_kernel(momentum, gradient, basis, weight, out):
    width = momentum.shape[1]
    rank = basis.shape[0]
    total = jnp.zeros((rank, 128), f32)
    pieces = []
    for start in range(0, width, 128):
        cut = slice(start, start + 128)
        buffer = decay_rate * momentum[:, cut] + gradient[:, cut]
        pieces.append(buffer)
        total = total + basis[:, cut] * buffer
    sums = jnp.broadcast_to(jnp.sum(total, axis=1, keepdims=True), (rank, 128))
    lane, sub = iota((rank, 128), 1), iota((rank, 128), 0)
    row = jnp.sum(jnp.where(lane % rank == sub, sums, 0.0), axis=0, keepdims=True)
    high, middle, low = three_parts(row)
    place = iota((1, 128), 1)
    coded = jnp.where(place < rank, high, jnp.where(place < 2 * rank, middle, jnp.where(place < 3 * rank, low, 0.0)))
    upper = jnp.concatenate(pieces + [coded], axis=1).astype(bf16)
    under = jnp.concatenate([weight[...], jnp.zeros((1, tail), bf16)], axis=1)
    both = jnp.concatenate([upper, under], axis=0)
    for peer in range(out.shape[0]):
        out[peer] = both


def second_kernel(upper_rows, out):
    rows = upper_rows.shape[0]
    width = upper_rows.shape[1] - tail
    rank = out.shape[1] - rows
    buffer = upper_rows[:, :width]
    square = lax.dot_general(buffer, buffer, (((1,), (1,)), ((), ())), preferred_element_type=f32)
    coded = upper_rows[:, width:].astype(f32).T
    power = coded[:rank] + coded[rank : 2 * rank] + coded[2 * rank : 3 * rank]
    for peer in range(out.shape[0]):
        out[peer, :rows] = square
        out[peer, rows:] = power


def third_kernel(
    scale, place, sums, upper_rows, weight_rows, momentum, gradient, inputs, new_momentum, new_basis, new_weight, activations
):
    rows, width = weight_rows.shape
    rank = new_basis.shape[0]
    total = sums[0]
    for peer in range(1, sums.shape[0]):
        total = total + sums[peer]
    square, power = total[:rows], total[rows:]
    gram = lax.dot_general(power, power, (((1,), (1,)), ((), ())), precision=highest, preferred_element_type=f32)
    sub = iota((rank, rows), 0)
    left = jnp.concatenate([gram, jnp.zeros((rank, rows - rank), f32)], axis=1)
    ortho = power
    for k in range(rank):
        column = jnp.broadcast_to(left[:, k : k + 1], (rank, rows))
        pivot = jnp.broadcast_to(column[k : k + 1], (rank, rows))
        root = 1.0 / jnp.sqrt(pivot)
        left_row = left[k : k + 1] * root
        ortho_row = ortho[k : k + 1] * root
        factor = column * root
        left = jnp.where(sub > k, left - factor * left_row, left)
        ortho = jnp.where(sub > k, ortho - factor * ortho_row, jnp.where(sub == k, ortho_row, ortho))
    along = lax.dot_general(ortho, square, (((1,), (0,)), ((), ())), precision=highest, preferred_element_type=f32)
    squares = jnp.maximum(jnp.sum(along * ortho, axis=1, keepdims=True), 0.0)
    inverse = 1.0 / jnp.sqrt(squares + epsilon)
    high, middle, low = three_parts(ortho)
    stacked = jnp.concatenate([high, middle, low], axis=0).astype(bf16)
    right_side = jnp.concatenate([high, high, middle, middle, high, low], axis=0)
    turned = jnp.concatenate([right_side, jnp.zeros((rows - 6 * rank, rows), f32)], axis=0).T.astype(bf16)
    here = place[0]
    own = jnp.sum(jnp.where(iota((rank, rows), 1) == here, ortho, 0.0), axis=1, keepdims=True) * (1.0 - decay_rate)
    chosen = (iota((16, rows), 1) == here).astype(f32).astype(bf16)
    left_side = jnp.concatenate([inputs[...], chosen], axis=0)
    chunk = 256
    for start in range(0, width, chunk):
        cut = slice(start, start + chunk)
        parts = jnp.dot(stacked, upper_rows[:, cut], preferred_element_type=f32)
        coeff = parts[:rank] + parts[rank : 2 * rank] + parts[2 * rank :]
        buffer = decay_rate * momentum[:, cut] + gradient[:, cut]
        new_momentum[:, cut] = buffer - jnp.sum(own * coeff, axis=0, keepdims=True)
        basis = coeff * inverse
        new_basis[:, cut] = basis
        high, middle, low = three_parts(basis)
        under = jnp.concatenate([high, middle, high, middle, low, high], axis=0).astype(bf16)
        step = jnp.dot(turned[:, : 6 * rank], under, preferred_element_type=f32)
        fresh = (weight_rows[:, cut].astype(f32) - scale * step).astype(bf16)
        result = jnp.dot(left_side, fresh, preferred_element_type=f32).astype(bf16)
        activations[:, cut] = result[: inputs.shape[0]]
        new_weight[:, cut] = result[inputs.shape[0] : inputs.shape[0] + 1]


vmem = pl.BlockSpec(memory_space=pltpu.VMEM)


def first_call(peers, momentum, gradient, basis, weight):
    return pl.pallas_call(
        first_kernel,
        out_shape=jax.ShapeDtypeStruct((peers, 2, momentum.shape[1] + tail), bf16),
        in_specs=[vmem] * 4,
        out_specs=vmem,
        name="first",
    )(momentum, gradient, basis, weight)


def second_call(peers, rank, upper_rows):
    rows = upper_rows.shape[0]
    return pl.pallas_call(
        second_kernel,
        out_shape=jax.ShapeDtypeStruct((peers, rows + rank, rows), f32),
        in_specs=[vmem],
        out_specs=vmem,
        name="second",
    )(upper_rows)


def third_call(scale, rank, place, sums, upper_rows, weight_rows, momentum, gradient, inputs):
    width = weight_rows.shape[1]
    return pl.pallas_call(
        functools.partial(third_kernel, scale),
        out_shape=(
            jax.ShapeDtypeStruct((1, width), f32),
            jax.ShapeDtypeStruct((rank, width), f32),
            jax.ShapeDtypeStruct((1, width), bf16),
            jax.ShapeDtypeStruct((inputs.shape[0], width), bf16),
        ),
        in_specs=[pl.BlockSpec(memory_space=pltpu.SMEM)] + [vmem] * 6,
        out_specs=(vmem,) * 4,
        name="third",
    )(place, sums, upper_rows, weight_rows, momentum, gradient, inputs)


def on_device(momentum, gradient, basis, weight, inputs):
    zh, zl, a = (lax.axis_size(n) for n in rows_axes)
    rows = zh * zl * a
    width = momentum.shape[1]
    rank = basis.shape[0]
    peers = lax.axis_size("tp")
    scale = step_size * math.sqrt(width * peers / rows)
    far = spread(first_call(zh, momentum, gradient, basis, weight), "zh")
    near = spread(replicated(far, "zl"), "zl").reshape(zl * zh, 2, width + tail)
    upper_rows = lax.all_gather(near[:, 0, :], "a", axis=0, tiled=True)
    weight_rows = lax.all_gather(near[:, 1, :width], "a", axis=0, tiled=True)
    sums = spread(second_call(peers, rank, upper_rows), "tp")
    place = (lax.axis_index("a") * zl + lax.axis_index("zl")) * zh + lax.axis_index("zh")
    ordered = inputs.reshape(-1, zh, zl, a).transpose(0, 3, 2, 1).reshape(-1, rows)
    return third_call(
        scale, rank, place.reshape(1).astype(jnp.int32), sums, upper_rows, weight_rows, momentum, gradient, ordered
    )


def solution(mesh):
    fsdp, tp = mesh.devices.shape
    fine = Mesh(mesh.devices.reshape(fsdp // 16, 4, 4, tp), rows_axes + ("tp",))
    return jax.shard_map(
        on_device,
        mesh=fine,
        in_specs=(
            P(rows_axes, "tp"),
            P(rows_axes, "tp"),
            P(None, "tp"),
            P(rows_axes, "tp"),
            P(rows_axes, None),
        ),
        out_specs=(P(rows_axes, "tp"), P(None, "tp"), P(rows_axes, "tp"), P(rows_axes, "tp")),
        check_vma=False,
    )
```

```python
import functools
import math

import jax
import jax.numpy as jnp
from jax import lax
from jax.experimental import pallas as pl
from jax.experimental.pallas import tpu as pltpu
from jax.sharding import Mesh, PartitionSpec as P

decay_rate = 0.8
step_size = 0.5
epsilon = 1e-06
highest = lax.Precision.HIGHEST
rows_axes = ("zh", "zl", "a")
tail = 128
bf16 = jnp.bfloat16
f32 = jnp.float32


def spread(blocks, axes):
    return lax.all_to_all(blocks, axes, 0, 0)


def replicated(block, axes):
    return jnp.broadcast_to(block[None], (lax.axis_size(axes),) + block.shape)


def iota(shape, dim):
    return lax.broadcasted_iota(jnp.int32, shape, dim)


def three_parts(x):
    high = x.astype(bf16).astype(f32)
    middle = (x - high).astype(bf16).astype(f32)
    return high, middle, x - high - middle


def inverse_root(x):
    guess = lax.rsqrt(x)
    return guess * (1.5 - 0.5 * x * guess * guess)


def first_kernel(momentum_hbm, gradient_hbm, basis_hbm, weight_hbm, out, momentum, gradient, basis, weight, arrived):
    pairs = ((momentum_hbm, momentum), (gradient_hbm, gradient), (basis_hbm, basis), (weight_hbm, weight))
    copies = [pltpu.make_async_copy(source, target, arrived.at[n]) for n, (source, target) in enumerate(pairs)]
    for copy in copies:
        copy.start()
    for copy in copies:
        copy.wait()
    width = momentum.shape[1]
    rank = basis.shape[0]
    total = jnp.zeros((rank, 128), f32)
    pieces = []
    for start in range(0, width, 128):
        cut = slice(start, start + 128)
        buffer = decay_rate * momentum[:, cut] + gradient[:, cut]
        pieces.append(buffer)
        total = total + basis[:, cut] * buffer
    sums = jnp.broadcast_to(jnp.sum(total, axis=1, keepdims=True), (rank, 128))
    lane, sub = iota((rank, 128), 1), iota((rank, 128), 0)
    row = jnp.sum(jnp.where(lane % rank == sub, sums, 0.0), axis=0, keepdims=True)
    high, middle, low = three_parts(row)
    place = iota((1, 128), 1)
    coded = jnp.where(place < rank, high, jnp.where(place < 2 * rank, middle, jnp.where(place < 3 * rank, low, 0.0)))
    upper = jnp.concatenate(pieces + [coded], axis=1).astype(bf16)
    under = jnp.concatenate([weight[...], jnp.zeros((1, tail), bf16)], axis=1)
    both = jnp.concatenate([upper, under], axis=0)
    for peer in range(out.shape[0]):
        out[peer] = both


def second_kernel(upper_rows, out):
    rows = upper_rows.shape[0]
    width = upper_rows.shape[1] - tail
    rank = out.shape[1] - rows
    buffer = upper_rows[:, :width]
    square = lax.dot_general(buffer, buffer, (((1,), (1,)), ((), ())), preferred_element_type=f32)
    coded = upper_rows[:, width:].astype(f32).T
    power = coded[:rank] + coded[rank : 2 * rank] + coded[2 * rank : 3 * rank]
    for peer in range(out.shape[0]):
        out[peer, :rows] = square
        out[peer, rows:] = power


def third_kernel(
    scale, place, sums, upper_rows, weight_rows, momentum, gradient, inputs, new_momentum, new_basis, new_weight, activations
):
    rows, width = weight_rows.shape
    rank = new_basis.shape[0]
    total = sums[0]
    for peer in range(1, sums.shape[0]):
        total = total + sums[peer]
    square, power = total[:rows], total[rows:]
    gram = lax.dot_general(power, power, (((1,), (1,)), ((), ())), precision=highest, preferred_element_type=f32)
    sub = iota((rank, rows), 0)
    columns = [jnp.broadcast_to(gram[:, k : k + 1], (rank, rows)) for k in range(rank)]
    ortho = power
    for k in range(rank):
        root = inverse_root(jnp.broadcast_to(columns[k][k : k + 1], (rank, rows)))
        factor = jnp.where(sub > k, columns[k] * root, 0.0)
        for j in range(k + 1, rank):
            columns[j] = columns[j] - factor * (columns[j][k : k + 1] * root[:1])
        ortho_row = ortho[k : k + 1] * root[:1]
        ortho = jnp.where(sub == k, ortho_row, ortho - factor * ortho_row)
    along = lax.dot_general(ortho, square, (((1,), (0,)), ((), ())), precision=highest, preferred_element_type=f32)
    squares = jnp.maximum(jnp.sum(along * ortho, axis=1, keepdims=True), 0.0)
    inverse = inverse_root(jnp.broadcast_to(squares, (rank, rows)) + epsilon)[:, :1]
    stacked = jnp.concatenate(three_parts(ortho), axis=0).astype(bf16)
    high, middle, low = three_parts(-scale * ortho)
    right_side = jnp.concatenate([high, high, middle, middle, high, low], axis=0)
    turned = jnp.concatenate([right_side, jnp.zeros((rows - 6 * rank, rows), f32)], axis=0).T.astype(bf16)
    identity = (iota((rows, rows), 0) == iota((rows, rows), 1)).astype(f32).astype(bf16)
    turned = jnp.concatenate([identity, turned], axis=1)
    here = place[0]
    own = jnp.sum(jnp.where(iota((rank, rows), 1) == here, ortho, 0.0), axis=1, keepdims=True) * (1.0 - decay_rate)
    chosen = (iota((16, rows), 1) == here).astype(f32).astype(bf16)
    left_side = jnp.concatenate([inputs[...], chosen], axis=0)
    chunk = 1664
    padding = jnp.zeros((rows - 6 * rank, chunk), f32)
    for start in range(0, width, chunk):
        cut = slice(start, start + chunk)
        parts = jnp.dot(stacked, upper_rows[:, cut], preferred_element_type=f32)
        coeff = parts[:rank] + parts[rank : 2 * rank] + parts[2 * rank :]
        buffer = decay_rate * momentum[:, cut] + gradient[:, cut]
        new_momentum[:, cut] = buffer - jnp.sum(own * coeff, axis=0, keepdims=True)
        basis = coeff * inverse
        new_basis[:, cut] = basis
        high, middle, low = three_parts(basis)
        under = jnp.concatenate([high, middle, high, middle, low, high, padding], axis=0).astype(bf16)
        mixed = jnp.concatenate([weight_rows[:, cut], under], axis=0)
        fresh = jnp.dot(turned, mixed, preferred_element_type=f32).astype(bf16)
        result = jnp.dot(left_side, fresh, preferred_element_type=f32).astype(bf16)
        activations[:, cut] = result[: inputs.shape[0]]
        new_weight[:, cut] = result[inputs.shape[0] : inputs.shape[0] + 1]


vmem = pl.BlockSpec(memory_space=pltpu.VMEM)
small_grant = pltpu.CompilerParams(vmem_limit_bytes=16 * 2**20)


def first_call(peers, momentum, gradient, basis, weight):
    arrays = [pltpu.with_memory_space_constraint(x, pltpu.HBM) for x in (momentum, gradient, basis, weight)]
    return pl.pallas_call(
        first_kernel,
        out_shape=jax.ShapeDtypeStruct((peers, 2, momentum.shape[1] + tail), bf16),
        in_specs=[pl.BlockSpec(memory_space=pltpu.HBM)] * 4,
        out_specs=vmem,
        scratch_shapes=[pltpu.VMEM(x.shape, x.dtype) for x in arrays] + [pltpu.SemaphoreType.DMA((4,))],
        compiler_params=small_grant,
        name="first",
    )(*arrays)


def second_call(peers, rank, upper_rows):
    rows = upper_rows.shape[0]
    return pl.pallas_call(
        second_kernel,
        out_shape=jax.ShapeDtypeStruct((peers, rows + rank, rows), f32),
        in_specs=[vmem],
        out_specs=vmem,
        compiler_params=small_grant,
        name="second",
    )(upper_rows)


def third_call(scale, rank, place, sums, upper_rows, weight_rows, momentum, gradient, inputs):
    width = weight_rows.shape[1]
    return pl.pallas_call(
        functools.partial(third_kernel, scale),
        out_shape=(
            jax.ShapeDtypeStruct((1, width), f32),
            jax.ShapeDtypeStruct((rank, width), f32),
            jax.ShapeDtypeStruct((1, width), bf16),
            jax.ShapeDtypeStruct((inputs.shape[0], width), bf16),
        ),
        in_specs=[pl.BlockSpec(memory_space=pltpu.SMEM)] + [vmem] * 6,
        out_specs=(vmem,) * 4,
        compiler_params=small_grant,
        name="third",
    )(place, sums, upper_rows, weight_rows, momentum, gradient, inputs)


def on_device(momentum, gradient, basis, weight, inputs):
    zh, zl, a = (lax.axis_size(n) for n in rows_axes)
    rows = zh * zl * a
    width = momentum.shape[1]
    rank = basis.shape[0]
    peers = lax.axis_size("tp")
    scale = step_size * math.sqrt(width * peers / rows)
    far = spread(first_call(zh, momentum, gradient, basis, weight), "zh")
    near = spread(replicated(far, "zl"), "zl").reshape(zl * zh, 2, width + tail)
    upper_rows = lax.all_gather(near[:, 0, :], "a", axis=0, tiled=True)
    weight_rows = lax.all_gather(near[:, 1, :width], "a", axis=0, tiled=True)
    sums = spread(second_call(peers, rank, upper_rows), "tp")
    place = (lax.axis_index("a") * zl + lax.axis_index("zl")) * zh + lax.axis_index("zh")
    ordered = inputs.reshape(-1, zh, zl, a).transpose(0, 3, 2, 1).reshape(-1, rows)
    return third_call(
        scale, rank, place.reshape(1).astype(jnp.int32), sums, upper_rows, weight_rows, momentum, gradient, ordered
    )


def solution(mesh):
    fsdp, tp = mesh.devices.shape
    fine = Mesh(mesh.devices.reshape(fsdp // 16, 4, 4, tp), rows_axes + ("tp",))
    return jax.shard_map(
        on_device,
        mesh=fine,
        in_specs=(
            P(rows_axes, "tp"),
            P(rows_axes, "tp"),
            P(None, "tp"),
            P(rows_axes, "tp"),
            P(rows_axes, None),
        ),
        out_specs=(P(rows_axes, "tp"), P(None, "tp"), P(rows_axes, "tp"), P(rows_axes, "tp")),
        check_vma=False,
    )
```

```python
import functools
import math

import jax
import jax.numpy as jnp
from jax import lax
from jax.experimental import pallas as pl
from jax.experimental.pallas import tpu as pltpu
from jax.sharding import Mesh, PartitionSpec as P

decay_rate = 0.8
step_size = 0.5
epsilon = 1e-06
highest = lax.Precision.HIGHEST
rows_axes = ("zh", "zl", "xl", "c")
tail = 128
bf16 = jnp.bfloat16
f32 = jnp.float32


def spread(blocks, axes):
    return lax.all_to_all(blocks, axes, 0, 0)


def replicated(block, axes):
    return jnp.broadcast_to(block[None], (lax.axis_size(axes),) + block.shape)


def iota(shape, dim):
    return lax.broadcasted_iota(jnp.int32, shape, dim)


def three_parts(x):
    high = x.astype(bf16).astype(f32)
    middle = (x - high).astype(bf16).astype(f32)
    return high, middle, x - high - middle


def inverse_root(x):
    guess = lax.rsqrt(x)
    return guess * (1.5 - 0.5 * x * guess * guess)


def first_kernel(momentum_hbm, gradient_hbm, basis_hbm, weight_hbm, out, momentum, gradient, basis, weight, arrived):
    pairs = ((momentum_hbm, momentum), (gradient_hbm, gradient), (basis_hbm, basis), (weight_hbm, weight))
    copies = [pltpu.make_async_copy(source, target, arrived.at[n]) for n, (source, target) in enumerate(pairs)]
    for copy in copies:
        copy.start()
    for copy in copies:
        copy.wait()
    width = momentum.shape[1]
    rank = basis.shape[0]
    total = jnp.zeros((rank, 128), f32)
    pieces = []
    for start in range(0, width, 128):
        cut = slice(start, start + 128)
        buffer = decay_rate * momentum[:, cut] + gradient[:, cut]
        pieces.append(buffer)
        total = total + basis[:, cut] * buffer
    sums = jnp.broadcast_to(jnp.sum(total, axis=1, keepdims=True), (rank, 128))
    lane, sub = iota((rank, 128), 1), iota((rank, 128), 0)
    row = jnp.sum(jnp.where(lane % rank == sub, sums, 0.0), axis=0, keepdims=True)
    high, middle, low = three_parts(row)
    place = iota((1, 128), 1)
    coded = jnp.where(place < rank, high, jnp.where(place < 2 * rank, middle, jnp.where(place < 3 * rank, low, 0.0)))
    upper = jnp.concatenate(pieces + [coded], axis=1).astype(bf16)
    under = jnp.concatenate([weight[...], jnp.zeros((1, tail), bf16)], axis=1)
    both = jnp.concatenate([upper, under], axis=0)
    for peer in range(out.shape[0]):
        out[peer] = both


def second_kernel(upper_rows, out):
    rows = upper_rows.shape[0]
    width = upper_rows.shape[1] - tail
    half, quarter = rows // 2, rows // 4
    rank = out.shape[1] - half - quarter
    buffer = upper_rows[:, :width]
    square = lax.dot_general(buffer, buffer, (((1,), (1,)), ((), ())), preferred_element_type=f32)
    corner = pltpu.roll(square[half + quarter :], quarter, 1)
    folded = jnp.where(iota((quarter, rows), 1) < quarter, corner, square[half : half + quarter])
    coded = upper_rows[:, width:].astype(f32).T
    power = coded[:rank] + coded[rank : 2 * rank] + coded[2 * rank : 3 * rank]
    for peer in range(out.shape[0]):
        out[peer, :half] = square[:half]
        out[peer, half : half + quarter] = folded
        out[peer, half + quarter :] = power


def quadratic(folded, vectors):
    rank, rows = vectors.shape
    half, quarter = rows // 2, rows // 4
    lane = iota((rank, rows), 1)
    in_third = (lane >= half) & (lane < half + quarter)
    turned = pltpu.roll(vectors, rows - quarter, 1)
    left = jnp.concatenate(
        [jnp.where(lane < half, vectors, 0.0), jnp.where(in_third, vectors, 0.0), jnp.where(in_third, turned, 0.0)], axis=0
    )
    right = jnp.concatenate([folded, jnp.zeros((quarter, rows), f32)], axis=0)
    along = lax.dot_general(left, right, (((1,), (0,)), ((), ())), precision=highest, preferred_element_type=f32)
    top = along[:rank] * vectors * jnp.where(lane < half, 1.0, 2.0)
    middle = along[rank : 2 * rank] * vectors * jnp.where(lane < half, 0.0, jnp.where(lane < half + quarter, 1.0, 2.0))
    corner = jnp.where(lane < quarter, along[2 * rank :] * pltpu.roll(vectors, quarter, 1), 0.0)
    return jnp.sum(top + middle + corner, axis=1, keepdims=True)


def third_kernel(
    scale, place, sums, upper_rows, weight_rows, momentum, gradient, inputs, new_momentum, new_basis, new_weight, activations
):
    rows, width = weight_rows.shape
    rank = new_basis.shape[0]
    total = sums[0]
    for peer in range(1, sums.shape[0]):
        total = total + sums[peer]
    folded, power = total[:-rank], total[-rank:]
    gram = lax.dot_general(power, power, (((1,), (1,)), ((), ())), precision=highest, preferred_element_type=f32)
    sub = iota((rank, rows), 0)
    columns = [jnp.broadcast_to(gram[:, k : k + 1], (rank, rows)) for k in range(rank)]
    ortho = power
    for k in range(rank):
        root = inverse_root(jnp.broadcast_to(columns[k][k : k + 1], (rank, rows)))
        factor = jnp.where(sub > k, columns[k] * root, 0.0)
        for j in range(k + 1, rank):
            columns[j] = columns[j] - factor * (columns[j][k : k + 1] * root[:1])
        ortho_row = ortho[k : k + 1] * root[:1]
        ortho = jnp.where(sub == k, ortho_row, ortho - factor * ortho_row)
    squares = jnp.maximum(quadratic(folded, ortho), 0.0)
    inverse = inverse_root(jnp.broadcast_to(squares, (rank, rows)) + epsilon)[:, :1]
    stacked = jnp.concatenate(three_parts(ortho), axis=0).astype(bf16)
    high, middle, low = three_parts(-scale * ortho)
    right_side = jnp.concatenate([high, high, middle, middle, high, low], axis=0)
    turned = jnp.concatenate([right_side, jnp.zeros((rows - 6 * rank, rows), f32)], axis=0).T.astype(bf16)
    here = place[0]
    own = jnp.sum(jnp.where(iota((rank, rows), 1) == here, ortho, 0.0), axis=1, keepdims=True) * (1.0 - decay_rate)
    chosen = (iota((16, rows), 1) == here).astype(f32).astype(bf16)
    left_side = jnp.concatenate([inputs[...], chosen], axis=0)
    parts = jnp.dot(stacked, upper_rows[:, :width], preferred_element_type=f32)
    coeff = parts[:rank] + parts[rank : 2 * rank] + parts[2 * rank :]
    buffer = decay_rate * momentum[...] + gradient[...]
    new_momentum[...] = buffer - jnp.sum(own * coeff, axis=0, keepdims=True)
    basis = coeff * inverse
    new_basis[...] = basis
    high, middle, low = three_parts(basis)
    under = jnp.concatenate([high, middle, high, middle, low, high], axis=0).astype(bf16)
    step = jnp.dot(turned[:, : 6 * rank], under, preferred_element_type=f32)
    fresh = (weight_rows[...].astype(f32) + step).astype(bf16)
    result = jnp.dot(left_side, fresh, preferred_element_type=f32).astype(bf16)
    activations[...] = result[: inputs.shape[0]]
    new_weight[...] = result[inputs.shape[0] : inputs.shape[0] + 1]


vmem = pl.BlockSpec(memory_space=pltpu.VMEM)
small_grant = pltpu.CompilerParams(vmem_limit_bytes=16 * 2**20)


def first_call(peers, momentum, gradient, basis, weight):
    arrays = [pltpu.with_memory_space_constraint(x, pltpu.HBM) for x in (momentum, gradient, basis, weight)]
    return pl.pallas_call(
        first_kernel,
        out_shape=jax.ShapeDtypeStruct((peers, 2, momentum.shape[1] + tail), bf16),
        in_specs=[pl.BlockSpec(memory_space=pltpu.HBM)] * 4,
        out_specs=vmem,
        scratch_shapes=[pltpu.VMEM(x.shape, x.dtype) for x in arrays] + [pltpu.SemaphoreType.DMA((4,))],
        compiler_params=small_grant,
        name="first",
    )(*arrays)


def second_call(peers, rank, upper_rows):
    rows = upper_rows.shape[0]
    return pl.pallas_call(
        second_kernel,
        out_shape=jax.ShapeDtypeStruct((peers, rows // 2 + rows // 4 + rank, rows), f32),
        in_specs=[vmem],
        out_specs=vmem,
        compiler_params=small_grant,
        name="second",
    )(upper_rows)


def third_call(scale, rank, place, sums, upper_rows, weight_rows, momentum, gradient, inputs):
    width = weight_rows.shape[1]
    return pl.pallas_call(
        functools.partial(third_kernel, scale),
        out_shape=(
            jax.ShapeDtypeStruct((1, width), f32),
            jax.ShapeDtypeStruct((rank, width), f32),
            jax.ShapeDtypeStruct((1, width), bf16),
            jax.ShapeDtypeStruct((inputs.shape[0], width), bf16),
        ),
        in_specs=[pl.BlockSpec(memory_space=pltpu.SMEM)] + [vmem] * 6,
        out_specs=(vmem,) * 4,
        compiler_params=small_grant,
        name="third",
    )(place, sums, upper_rows, weight_rows, momentum, gradient, inputs)


def on_device(momentum, gradient, basis, weight, inputs):
    zh, zl, xl, c = (lax.axis_size(n) for n in rows_axes)
    rows = zh * zl * xl * c
    width = momentum.shape[1]
    rank = basis.shape[0]
    peers = lax.axis_size("tp")
    scale = step_size * math.sqrt(width * peers / rows)
    far = spread(first_call(zh, momentum, gradient, basis, weight), "zh")
    near = spread(replicated(far, ("zl", "xl")), ("zl", "xl")).reshape(zl * xl * zh, 2, width + tail)
    upper_rows = lax.all_gather(near[:, 0, :], "c", axis=0, tiled=True)
    weight_rows = lax.all_gather(near[:, 1, :width], "c", axis=0, tiled=True)
    sums = spread(second_call(peers, rank, upper_rows), "tp")
    place = ((lax.axis_index("c") * zl + lax.axis_index("zl")) * xl + lax.axis_index("xl")) * zh + lax.axis_index("zh")
    ordered = inputs.reshape(-1, zh, zl, xl, c).transpose(0, 4, 2, 3, 1).reshape(-1, rows)
    return third_call(
        scale, rank, place.reshape(1).astype(jnp.int32), sums, upper_rows, weight_rows, momentum, gradient, ordered
    )


def solution(mesh):
    fsdp, tp = mesh.devices.shape
    fine = Mesh(mesh.devices.reshape(fsdp // 16, 4, 2, 2, tp), rows_axes + ("tp",))
    return jax.shard_map(
        on_device,
        mesh=fine,
        in_specs=(
            P(rows_axes, "tp"),
            P(rows_axes, "tp"),
            P(None, "tp"),
            P(rows_axes, "tp"),
            P(rows_axes, None),
        ),
        out_specs=(P(rows_axes, "tp"), P(None, "tp"), P(rows_axes, "tp"), P(rows_axes, "tp")),
        check_vma=False,
    )
```

```python
import functools
import math

import jax
import jax.numpy as jnp
from jax import lax
from jax.experimental import pallas as pl
from jax.experimental.pallas import tpu as pltpu
from jax.sharding import Mesh, PartitionSpec as P

decay_rate = 0.8
step_size = 0.5
epsilon = 1e-06
highest = lax.Precision.HIGHEST
rows_axes = ("zh", "zl", "a")
tail = 128
bf16 = jnp.bfloat16
f32 = jnp.float32


def spread(blocks, axes):
    return lax.all_to_all(blocks, axes, 0, 0)


def replicated(block, axes):
    return jnp.broadcast_to(block[None], (lax.axis_size(axes),) + block.shape)


def iota(shape, dim):
    return lax.broadcasted_iota(jnp.int32, shape, dim)


def three_parts(x):
    high = x.astype(bf16).astype(f32)
    middle = (x - high).astype(bf16).astype(f32)
    return high, middle, x - high - middle


def inverse_root(x):
    guess = lax.rsqrt(x)
    return guess * (1.5 - 0.5 * x * guess * guess)


def first_kernel(momentum_hbm, gradient_hbm, basis_hbm, weight_hbm, out, momentum, gradient, basis, weight, arrived):
    pairs = ((momentum_hbm, momentum), (gradient_hbm, gradient), (basis_hbm, basis), (weight_hbm, weight))
    copies = [pltpu.make_async_copy(source, target, arrived.at[n]) for n, (source, target) in enumerate(pairs)]
    for copy in copies:
        copy.start()
    for copy in copies:
        copy.wait()
    width = momentum.shape[1]
    rank = basis.shape[0]
    total = jnp.zeros((rank, 128), f32)
    pieces = []
    for start in range(0, width, 128):
        cut = slice(start, start + 128)
        buffer = decay_rate * momentum[:, cut] + gradient[:, cut]
        pieces.append(buffer)
        total = total + basis[:, cut] * buffer
    sums = jnp.broadcast_to(jnp.sum(total, axis=1, keepdims=True), (rank, 128))
    lane, sub = iota((rank, 128), 1), iota((rank, 128), 0)
    row = jnp.sum(jnp.where(lane % rank == sub, sums, 0.0), axis=0, keepdims=True)
    high, middle, low = three_parts(row)
    place = iota((1, 128), 1)
    coded = jnp.where(place < rank, high, jnp.where(place < 2 * rank, middle, jnp.where(place < 3 * rank, low, 0.0)))
    upper = jnp.concatenate(pieces + [coded], axis=1).astype(bf16)
    under = jnp.concatenate([weight[...], jnp.zeros((1, tail), bf16)], axis=1)
    both = jnp.concatenate([upper, under], axis=0)
    for peer in range(out.shape[0]):
        out[peer] = both


def second_kernel(upper_rows, out):
    rows = upper_rows.shape[0]
    width = upper_rows.shape[1] - tail
    half, quarter = rows // 2, rows // 4
    rank = out.shape[1] - half - quarter
    buffer = upper_rows[:, :width]
    square = lax.dot_general(buffer, buffer, (((1,), (1,)), ((), ())), preferred_element_type=f32)
    corner = pltpu.roll(square[half + quarter :], quarter, 1)
    folded = jnp.where(iota((quarter, rows), 1) < quarter, corner, square[half : half + quarter])
    coded = upper_rows[:, width:].astype(f32).T
    power = coded[:rank] + coded[rank : 2 * rank] + coded[2 * rank : 3 * rank]
    for peer in range(out.shape[0]):
        out[peer, :half] = square[:half]
        out[peer, half : half + quarter] = folded
        out[peer, half + quarter :] = power


def quadratic(folded, vectors):
    rank, rows = vectors.shape
    half, quarter = rows // 2, rows // 4
    lane = iota((rank, rows), 1)
    in_third = (lane >= half) & (lane < half + quarter)
    turned = pltpu.roll(vectors, rows - quarter, 1)
    left = jnp.concatenate(
        [jnp.where(lane < half, vectors, 0.0), jnp.where(in_third, vectors, 0.0), jnp.where(in_third, turned, 0.0)], axis=0
    )
    right = jnp.concatenate([folded, jnp.zeros((quarter, rows), f32)], axis=0)
    along = lax.dot_general(left, right, (((1,), (0,)), ((), ())), precision=highest, preferred_element_type=f32)
    top = along[:rank] * vectors * jnp.where(lane < half, 1.0, 2.0)
    middle = along[rank : 2 * rank] * vectors * jnp.where(lane < half, 0.0, jnp.where(lane < half + quarter, 1.0, 2.0))
    corner = jnp.where(lane < quarter, along[2 * rank :] * pltpu.roll(vectors, quarter, 1), 0.0)
    return jnp.sum(top + middle + corner, axis=1, keepdims=True)


def third_kernel(
    scale, place, sums, upper_rows, weight_rows, momentum, gradient, inputs, new_momentum, new_basis, new_weight, activations
):
    rows, width = weight_rows.shape
    rank = new_basis.shape[0]
    total = sums[0]
    for peer in range(1, sums.shape[0]):
        total = total + sums[peer]
    folded, power = total[:-rank], total[-rank:]
    gram = lax.dot_general(power, power, (((1,), (1,)), ((), ())), precision=highest, preferred_element_type=f32)
    sub = iota((rank, rows), 0)
    columns = [jnp.broadcast_to(gram[:, k : k + 1], (rank, rows)) for k in range(rank)]
    ortho = power
    for k in range(rank):
        root = inverse_root(jnp.broadcast_to(columns[k][k : k + 1], (rank, rows)))
        factor = jnp.where(sub > k, columns[k] * root, 0.0)
        for j in range(k + 1, rank):
            columns[j] = columns[j] - factor * (columns[j][k : k + 1] * root[:1])
        ortho_row = ortho[k : k + 1] * root[:1]
        ortho = jnp.where(sub == k, ortho_row, ortho - factor * ortho_row)
    squares = jnp.maximum(quadratic(folded, ortho), 0.0)
    inverse = inverse_root(jnp.broadcast_to(squares, (rank, rows)) + epsilon)[:, :1]
    stacked = jnp.concatenate(three_parts(ortho), axis=0).astype(bf16)
    high, middle, low = three_parts(-scale * ortho)
    right_side = jnp.concatenate([high, high, middle, middle, high, low], axis=0)
    turned = jnp.concatenate([right_side, jnp.zeros((rows - 6 * rank, rows), f32)], axis=0).T.astype(bf16)
    here = place[0]
    own = jnp.sum(jnp.where(iota((rank, rows), 1) == here, ortho, 0.0), axis=1, keepdims=True) * (1.0 - decay_rate)
    chosen = (iota((16, rows), 1) == here).astype(f32).astype(bf16)
    left_side = jnp.concatenate([inputs[...], chosen], axis=0)
    parts = jnp.dot(stacked, upper_rows[:, :width], preferred_element_type=f32)
    coeff = parts[:rank] + parts[rank : 2 * rank] + parts[2 * rank :]
    buffer = decay_rate * momentum[...] + gradient[...]
    new_momentum[...] = buffer - jnp.sum(own * coeff, axis=0, keepdims=True)
    basis = coeff * inverse
    new_basis[...] = basis
    high, middle, low = three_parts(basis)
    under = jnp.concatenate([high, middle, high, middle, low, high], axis=0).astype(bf16)
    step = jnp.dot(turned[:, : 6 * rank], under, preferred_element_type=f32)
    fresh = (weight_rows[...].astype(f32) + step).astype(bf16)
    result = jnp.dot(left_side, fresh, preferred_element_type=f32).astype(bf16)
    activations[...] = result[: inputs.shape[0]]
    new_weight[...] = result[inputs.shape[0] : inputs.shape[0] + 1]


vmem = pl.BlockSpec(memory_space=pltpu.VMEM)
small_grant = pltpu.CompilerParams(vmem_limit_bytes=16 * 2**20)


def first_call(peers, momentum, gradient, basis, weight):
    arrays = [pltpu.with_memory_space_constraint(x, pltpu.HBM) for x in (momentum, gradient, basis, weight)]
    return pl.pallas_call(
        first_kernel,
        out_shape=jax.ShapeDtypeStruct((peers, 2, momentum.shape[1] + tail), bf16),
        in_specs=[pl.BlockSpec(memory_space=pltpu.HBM)] * 4,
        out_specs=vmem,
        scratch_shapes=[pltpu.VMEM(x.shape, x.dtype) for x in arrays] + [pltpu.SemaphoreType.DMA((4,))],
        compiler_params=small_grant,
        name="first",
    )(*arrays)


def second_call(peers, rank, upper_rows):
    rows = upper_rows.shape[0]
    return pl.pallas_call(
        second_kernel,
        out_shape=jax.ShapeDtypeStruct((peers, rows // 2 + rows // 4 + rank, rows), f32),
        in_specs=[vmem],
        out_specs=vmem,
        compiler_params=small_grant,
        name="second",
    )(upper_rows)


def third_call(scale, rank, place, sums, upper_rows, weight_rows, momentum, gradient, inputs):
    width = weight_rows.shape[1]
    return pl.pallas_call(
        functools.partial(third_kernel, scale),
        out_shape=(
            jax.ShapeDtypeStruct((1, width), f32),
            jax.ShapeDtypeStruct((rank, width), f32),
            jax.ShapeDtypeStruct((1, width), bf16),
            jax.ShapeDtypeStruct((inputs.shape[0], width), bf16),
        ),
        in_specs=[pl.BlockSpec(memory_space=pltpu.SMEM)] + [vmem] * 6,
        out_specs=(vmem,) * 4,
        compiler_params=small_grant,
        name="third",
    )(place, sums, upper_rows, weight_rows, momentum, gradient, inputs)


def on_device(momentum, gradient, basis, weight, inputs):
    zh, zl, a = (lax.axis_size(n) for n in rows_axes)
    rows = zh * zl * a
    width = momentum.shape[1]
    rank = basis.shape[0]
    peers = lax.axis_size("tp")
    scale = step_size * math.sqrt(width * peers / rows)
    far = spread(first_call(zh, momentum, gradient, basis, weight), "zh")
    near = spread(replicated(far, "zl"), "zl").reshape(zl * zh, 2, width + tail)
    upper_rows = lax.all_gather(near[:, 0, :], "a", axis=0, tiled=True)
    weight_rows = lax.all_gather(near[:, 1, :width], "a", axis=0, tiled=True)
    sums = spread(second_call(peers, rank, upper_rows), "tp")
    place = (lax.axis_index("a") * zl + lax.axis_index("zl")) * zh + lax.axis_index("zh")
    ordered = inputs.reshape(-1, zh, zl, a).transpose(0, 3, 2, 1).reshape(-1, rows)
    return third_call(
        scale, rank, place.reshape(1).astype(jnp.int32), sums, upper_rows, weight_rows, momentum, gradient, ordered
    )


def solution(mesh):
    fsdp, tp = mesh.devices.shape
    fine = Mesh(mesh.devices.reshape(fsdp // 16, 4, 4, tp), rows_axes + ("tp",))
    return jax.shard_map(
        on_device,
        mesh=fine,
        in_specs=(
            P(rows_axes, "tp"),
            P(rows_axes, "tp"),
            P(None, "tp"),
            P(rows_axes, "tp"),
            P(rows_axes, None),
        ),
        out_specs=(P(rows_axes, "tp"), P(None, "tp"), P(rows_axes, "tp"), P(rows_axes, "tp")),
        check_vma=False,
    )
```

```python
import functools
import math

import jax
import jax.numpy as jnp
from jax import lax
from jax.experimental import pallas as pl
from jax.experimental.pallas import tpu as pltpu
from jax.sharding import Mesh, PartitionSpec as P

decay_rate = 0.8
step_size = 0.5
epsilon = 1e-06
highest = lax.Precision.HIGHEST
rows_axes = ("zh", "zl", "xl", "c")
tail = 128
bf16 = jnp.bfloat16
f32 = jnp.float32


def spread(blocks, axes):
    return lax.all_to_all(blocks, axes, 0, 0)


def replicated(block, axes):
    return jnp.broadcast_to(block[None], (lax.axis_size(axes),) + block.shape)


def iota(shape, dim):
    return lax.broadcasted_iota(jnp.int32, shape, dim)


def three_parts(x):
    high = x.astype(bf16).astype(f32)
    middle = (x - high).astype(bf16).astype(f32)
    return high, middle, x - high - middle


def inverse_root(x):
    guess = lax.rsqrt(x)
    return guess * (1.5 - 0.5 * x * guess * guess)


def first_kernel(momentum_hbm, gradient_hbm, basis_hbm, weight_hbm, out, momentum, gradient, basis, weight, arrived):
    pairs = ((momentum_hbm, momentum), (gradient_hbm, gradient), (basis_hbm, basis), (weight_hbm, weight))
    copies = [pltpu.make_async_copy(source, target, arrived.at[n]) for n, (source, target) in enumerate(pairs)]
    for copy in copies:
        copy.start()
    for copy in copies:
        copy.wait()
    width = momentum.shape[1]
    rank = basis.shape[0]
    total = jnp.zeros((rank, 128), f32)
    pieces = []
    for start in range(0, width, 128):
        cut = slice(start, start + 128)
        buffer = decay_rate * momentum[:, cut] + gradient[:, cut]
        pieces.append(buffer)
        total = total + basis[:, cut] * buffer
    sums = jnp.broadcast_to(jnp.sum(total, axis=1, keepdims=True), (rank, 128))
    lane, sub = iota((rank, 128), 1), iota((rank, 128), 0)
    row = jnp.sum(jnp.where(lane % rank == sub, sums, 0.0), axis=0, keepdims=True)
    high, middle, low = three_parts(row)
    place = iota((1, 128), 1)
    coded = jnp.where(place < rank, high, jnp.where(place < 2 * rank, middle, jnp.where(place < 3 * rank, low, 0.0)))
    upper = jnp.concatenate(pieces + [coded], axis=1).astype(bf16)
    under = jnp.concatenate([weight[...], jnp.zeros((1, tail), bf16)], axis=1)
    both = jnp.concatenate([upper, under], axis=0)
    for peer in range(out.shape[0]):
        out[peer] = both


def second_kernel(upper_rows, out):
    rows = upper_rows.shape[0]
    width = upper_rows.shape[1] - tail
    half, quarter = rows // 2, rows // 4
    rank = out.shape[1] - half - quarter
    buffer = upper_rows[:, :width]
    square = lax.dot_general(buffer, buffer, (((1,), (1,)), ((), ())), preferred_element_type=f32)
    corner = pltpu.roll(square[half + quarter :], quarter, 1)
    folded = jnp.where(iota((quarter, rows), 1) < quarter, corner, square[half : half + quarter])
    coded = upper_rows[:, width:].astype(f32).T
    power = coded[:rank] + coded[rank : 2 * rank] + coded[2 * rank : 3 * rank]
    for peer in range(out.shape[0]):
        out[peer, :half] = square[:half]
        out[peer, half : half + quarter] = folded
        out[peer, half + quarter :] = power


def quadratic(folded, vectors):
    rank, rows = vectors.shape
    half, quarter = rows // 2, rows // 4
    lane = iota((rank, rows), 1)
    in_third = (lane >= half) & (lane < half + quarter)
    turned = pltpu.roll(vectors, rows - quarter, 1)
    left = jnp.concatenate(
        [jnp.where(lane < half, vectors, 0.0), jnp.where(in_third, vectors, 0.0), jnp.where(in_third, turned, 0.0)], axis=0
    )
    right = jnp.concatenate([folded, jnp.zeros((quarter, rows), f32)], axis=0)
    along = lax.dot_general(left, right, (((1,), (0,)), ((), ())), precision=highest, preferred_element_type=f32)
    top = along[:rank] * vectors * jnp.where(lane < half, 1.0, 2.0)
    middle = along[rank : 2 * rank] * vectors * jnp.where(lane < half, 0.0, jnp.where(lane < half + quarter, 1.0, 2.0))
    corner = jnp.where(lane < quarter, along[2 * rank :] * pltpu.roll(vectors, quarter, 1), 0.0)
    return jnp.sum(top + middle + corner, axis=1, keepdims=True)


def third_kernel(
    scale, place, side, sums, upper_rows, weight_rows, momentum, gradient, inputs, new_momentum, new_basis, new_weight, activations
):
    rows, width = weight_rows.shape
    rank = new_basis.shape[0]
    total = sums[0]
    for peer in range(1, sums.shape[0]):
        total = total + sums[peer]
    folded, power = total[:-rank], total[-rank:]
    gram = lax.dot_general(power, power, (((1,), (1,)), ((), ())), precision=highest, preferred_element_type=f32)
    sub = iota((rank, rows), 0)
    columns = [jnp.broadcast_to(gram[:, k : k + 1], (rank, rows)) for k in range(rank)]
    ortho = power
    for k in range(rank):
        root = inverse_root(jnp.broadcast_to(columns[k][k : k + 1], (rank, rows)))
        factor = jnp.where(sub > k, columns[k] * root, 0.0)
        for j in range(k + 1, rank):
            columns[j] = columns[j] - factor * (columns[j][k : k + 1] * root[:1])
        ortho_row = ortho[k : k + 1] * root[:1]
        ortho = jnp.where(sub == k, ortho_row, ortho - factor * ortho_row)
    squares = jnp.maximum(quadratic(folded, ortho), 0.0)
    inverse = inverse_root(jnp.broadcast_to(squares, (rank, rows)) + epsilon)[:, :1]
    stacked = jnp.concatenate(three_parts(ortho), axis=0).astype(bf16)
    high, middle, low = three_parts(-scale * ortho)
    right_side = jnp.concatenate([high, high, middle, middle, high, low], axis=0)
    turned = jnp.concatenate([right_side, jnp.zeros((rows - 6 * rank, rows), f32)], axis=0).T.astype(bf16)
    here = place[0]
    own = jnp.sum(jnp.where(iota((rank, rows), 1) == here, ortho, 0.0), axis=1, keepdims=True) * (1.0 - decay_rate)
    chosen = (iota((16, rows), 1) == here).astype(f32).astype(bf16)
    left_side = jnp.concatenate([inputs[...], chosen], axis=0)
    parts = jnp.dot(stacked, upper_rows[:, :width], preferred_element_type=f32)
    coeff = parts[:rank] + parts[rank : 2 * rank] + parts[2 * rank :]
    buffer = decay_rate * momentum[...] + gradient[...]
    new_momentum[...] = buffer - jnp.sum(own * coeff, axis=0, keepdims=True)
    basis = coeff * inverse
    new_basis[...] = basis
    high, middle, low = three_parts(basis)
    under = jnp.concatenate([high, middle, high, middle, low, high], axis=0).astype(bf16)
    step = jnp.dot(turned[:, : 6 * rank], under, preferred_element_type=f32)
    block = rows // 4
    starts = [core * 2 * block + (at_x ^ side[0]) * block for at_x in range(2) for core in range(2)]
    held = jnp.concatenate([weight_rows[pl.ds(pl.multiple_of(start, block), block), :] for start in starts], axis=0)
    fresh = (held.astype(f32) + step).astype(bf16)
    result = jnp.dot(left_side, fresh, preferred_element_type=f32).astype(bf16)
    activations[...] = result[: inputs.shape[0]]
    new_weight[...] = result[inputs.shape[0] : inputs.shape[0] + 1]


vmem = pl.BlockSpec(memory_space=pltpu.VMEM)
small_grant = pltpu.CompilerParams(vmem_limit_bytes=16 * 2**20)


def first_call(peers, momentum, gradient, basis, weight):
    arrays = [pltpu.with_memory_space_constraint(x, pltpu.HBM) for x in (momentum, gradient, basis, weight)]
    return pl.pallas_call(
        first_kernel,
        out_shape=jax.ShapeDtypeStruct((peers, 2, momentum.shape[1] + tail), bf16),
        in_specs=[pl.BlockSpec(memory_space=pltpu.HBM)] * 4,
        out_specs=vmem,
        scratch_shapes=[pltpu.VMEM(x.shape, x.dtype) for x in arrays] + [pltpu.SemaphoreType.DMA((4,))],
        compiler_params=small_grant,
        name="first",
    )(*arrays)


def second_call(peers, rank, upper_rows):
    rows = upper_rows.shape[0]
    return pl.pallas_call(
        second_kernel,
        out_shape=jax.ShapeDtypeStruct((peers, rows // 2 + rows // 4 + rank, rows), f32),
        in_specs=[vmem],
        out_specs=vmem,
        compiler_params=small_grant,
        name="second",
    )(upper_rows)


def third_call(scale, rank, place, side, sums, upper_rows, weight_rows, momentum, gradient, inputs):
    width = weight_rows.shape[1]
    return pl.pallas_call(
        functools.partial(third_kernel, scale),
        out_shape=(
            jax.ShapeDtypeStruct((1, width), f32),
            jax.ShapeDtypeStruct((rank, width), f32),
            jax.ShapeDtypeStruct((1, width), bf16),
            jax.ShapeDtypeStruct((inputs.shape[0], width), bf16),
        ),
        in_specs=[pl.BlockSpec(memory_space=pltpu.SMEM)] * 2 + [vmem] * 6,
        out_specs=(vmem,) * 4,
        compiler_params=small_grant,
        name="third",
    )(place, side, sums, upper_rows, weight_rows, momentum, gradient, inputs)


def on_device(momentum, gradient, basis, weight, inputs):
    zh, zl, xl, c = (lax.axis_size(n) for n in rows_axes)
    rows = zh * zl * xl * c
    width = momentum.shape[1]
    rank = basis.shape[0]
    peers = lax.axis_size("tp")
    scale = step_size * math.sqrt(width * peers / rows)
    far = spread(first_call(zh, momentum, gradient, basis, weight), "zh")
    near = spread(replicated(far, "zl"), "zl").reshape(zl * zh, 2, width + tail)
    upper_rows = lax.all_gather(near[:, 0, :], ("xl", "c"), axis=0, tiled=True)
    weight_near, upper_rows = lax.optimization_barrier((near[:, 1, :width], upper_rows))
    across = lax.ppermute(weight_near, "xl", [(0, 1), (1, 0)])
    sums = spread(second_call(peers, rank, upper_rows), "tp")
    weight_rows = lax.all_gather(jnp.concatenate([weight_near, across], axis=0), "c", axis=0, tiled=True)
    at_x = lax.axis_index("xl")
    place = ((at_x * c + lax.axis_index("c")) * zl + lax.axis_index("zl")) * zh + lax.axis_index("zh")
    ordered = inputs.reshape(-1, zh, zl, xl, c).transpose(0, 3, 4, 2, 1).reshape(-1, rows)
    place, side = (x.reshape(1).astype(jnp.int32) for x in (place, at_x))
    return third_call(scale, rank, place, side, sums, upper_rows, weight_rows, momentum, gradient, ordered)


def solution(mesh):
    fsdp, tp = mesh.devices.shape
    fine = Mesh(mesh.devices.reshape(fsdp // 16, 4, 2, 2, tp), rows_axes + ("tp",))
    return jax.shard_map(
        on_device,
        mesh=fine,
        in_specs=(
            P(rows_axes, "tp"),
            P(rows_axes, "tp"),
            P(None, "tp"),
            P(rows_axes, "tp"),
            P(rows_axes, None),
        ),
        out_specs=(P(rows_axes, "tp"), P(None, "tp"), P(rows_axes, "tp"), P(rows_axes, "tp")),
        check_vma=False,
    )
```

```python
import functools
import math

import jax
import jax.numpy as jnp
from jax import lax
from jax.experimental import pallas as pl
from jax.experimental.pallas import tpu as pltpu
from jax.sharding import Mesh, PartitionSpec as P

decay_rate = 0.8
step_size = 0.5
epsilon = 1e-06
highest = lax.Precision.HIGHEST
rows_axes = ("zh", "zl", "a")
tail = 128
bf16 = jnp.bfloat16
f32 = jnp.float32


def spread(blocks, axes):
    return lax.all_to_all(blocks, axes, 0, 0)


def replicated(block, axes):
    return jnp.broadcast_to(block[None], (lax.axis_size(axes),) + block.shape)


def iota(shape, dim):
    return lax.broadcasted_iota(jnp.int32, shape, dim)


def three_parts(x):
    high = x.astype(bf16).astype(f32)
    middle = (x - high).astype(bf16).astype(f32)
    return high, middle, x - high - middle


def inverse_root(x):
    guess = lax.rsqrt(x)
    return guess * (1.5 - 0.5 * x * guess * guess)


def first_kernel(momentum_hbm, gradient_hbm, basis_hbm, weight_hbm, out, momentum, gradient, basis, weight, arrived):
    pairs = ((momentum_hbm, momentum), (gradient_hbm, gradient), (basis_hbm, basis), (weight_hbm, weight))
    copies = [pltpu.make_async_copy(source, target, arrived.at[n]) for n, (source, target) in enumerate(pairs)]
    for copy in copies:
        copy.start()
    for copy in copies:
        copy.wait()
    width = momentum.shape[1]
    rank = basis.shape[0]
    total = jnp.zeros((rank, 128), f32)
    pieces = []
    for start in range(0, width, 128):
        cut = slice(start, start + 128)
        buffer = decay_rate * momentum[:, cut] + gradient[:, cut]
        pieces.append(buffer)
        total = total + basis[:, cut] * buffer
    sums = jnp.broadcast_to(jnp.sum(total, axis=1, keepdims=True), (rank, 128))
    lane, sub = iota((rank, 128), 1), iota((rank, 128), 0)
    row = jnp.sum(jnp.where(lane % rank == sub, sums, 0.0), axis=0, keepdims=True)
    high, middle, low = three_parts(row)
    place = iota((1, 128), 1)
    coded = jnp.where(place < rank, high, jnp.where(place < 2 * rank, middle, jnp.where(place < 3 * rank, low, 0.0)))
    upper = jnp.concatenate(pieces + [coded], axis=1).astype(bf16)
    under = jnp.concatenate([weight[...], jnp.zeros((1, tail), bf16)], axis=1)
    both = jnp.concatenate([upper, under], axis=0)
    for peer in range(out.shape[0]):
        out[peer] = both


def second_kernel(upper_rows, out):
    rows = upper_rows.shape[0]
    width = upper_rows.shape[1] - tail
    half, quarter = rows // 2, rows // 4
    rank = out.shape[1] - half - quarter
    buffer = upper_rows[:, :width]
    square = lax.dot_general(buffer, buffer, (((1,), (1,)), ((), ())), preferred_element_type=f32)
    corner = pltpu.roll(square[half + quarter :], quarter, 1)
    folded = jnp.where(iota((quarter, rows), 1) < quarter, corner, square[half : half + quarter])
    coded = upper_rows[:, width:].astype(f32).T
    power = coded[:rank] + coded[rank : 2 * rank] + coded[2 * rank : 3 * rank]
    for peer in range(out.shape[0]):
        out[peer, :half] = square[:half]
        out[peer, half : half + quarter] = folded
        out[peer, half + quarter :] = power


def quadratic(folded, vectors):
    rank, rows = vectors.shape
    half, quarter = rows // 2, rows // 4
    lane = iota((rank, rows), 1)
    in_third = (lane >= half) & (lane < half + quarter)
    turned = pltpu.roll(vectors, rows - quarter, 1)
    left = jnp.concatenate(
        [jnp.where(lane < half, vectors, 0.0), jnp.where(in_third, vectors, 0.0), jnp.where(in_third, turned, 0.0)], axis=0
    )
    right = jnp.concatenate([folded, jnp.zeros((quarter, rows), f32)], axis=0)
    along = lax.dot_general(left, right, (((1,), (0,)), ((), ())), precision=highest, preferred_element_type=f32)
    top = along[:rank] * vectors * jnp.where(lane < half, 1.0, 2.0)
    middle = along[rank : 2 * rank] * vectors * jnp.where(lane < half, 0.0, jnp.where(lane < half + quarter, 1.0, 2.0))
    corner = jnp.where(lane < quarter, along[2 * rank :] * pltpu.roll(vectors, quarter, 1), 0.0)
    return jnp.sum(top + middle + corner, axis=1, keepdims=True)


def third_kernel(
    scale, near_size, place, layer, sums, upper_rows, weight_rows, momentum, gradient, inputs, new_momentum, new_basis, new_weight, activations
):
    rows, width = weight_rows.shape
    rank = new_basis.shape[0]
    total = sums[0]
    for peer in range(1, sums.shape[0]):
        total = total + sums[peer]
    folded, power = total[:-rank], total[-rank:]
    gram = lax.dot_general(power, power, (((1,), (1,)), ((), ())), precision=highest, preferred_element_type=f32)
    sub = iota((rank, rows), 0)
    columns = [jnp.broadcast_to(gram[:, k : k + 1], (rank, rows)) for k in range(rank)]
    ortho = power
    for k in range(rank):
        root = inverse_root(jnp.broadcast_to(columns[k][k : k + 1], (rank, rows)))
        factor = jnp.where(sub > k, columns[k] * root, 0.0)
        for j in range(k + 1, rank):
            columns[j] = columns[j] - factor * (columns[j][k : k + 1] * root[:1])
        ortho_row = ortho[k : k + 1] * root[:1]
        ortho = jnp.where(sub == k, ortho_row, ortho - factor * ortho_row)
    squares = jnp.maximum(quadratic(folded, ortho), 0.0)
    inverse = inverse_root(jnp.broadcast_to(squares, (rank, rows)) + epsilon)[:, :1]
    stacked = jnp.concatenate(three_parts(ortho), axis=0).astype(bf16)
    high, middle, low = three_parts(-scale * ortho)
    right_side = jnp.concatenate([high, high, middle, middle, high, low], axis=0)
    turned = jnp.concatenate([right_side, jnp.zeros((rows - 6 * rank, rows), f32)], axis=0).T.astype(bf16)
    here = place[0]
    own = jnp.sum(jnp.where(iota((rank, rows), 1) == here, ortho, 0.0), axis=1, keepdims=True) * (1.0 - decay_rate)
    chosen = (iota((16, rows), 1) == here).astype(f32).astype(bf16)
    left_side = jnp.concatenate([inputs[...], chosen], axis=0)
    parts = jnp.dot(stacked, upper_rows[:, :width], preferred_element_type=f32)
    coeff = parts[:rank] + parts[rank : 2 * rank] + parts[2 * rank :]
    buffer = decay_rate * momentum[...] + gradient[...]
    new_momentum[...] = buffer - jnp.sum(own * coeff, axis=0, keepdims=True)
    basis = coeff * inverse
    new_basis[...] = basis
    high, middle, low = three_parts(basis)
    under = jnp.concatenate([high, middle, high, middle, low, high], axis=0).astype(bf16)
    step = jnp.dot(turned[:, : 6 * rank], under, preferred_element_type=f32)
    groups, layers, size = near_size
    starts = [(g * layers + lax.rem(layer[0] - n + layers, layers)) * size for g in range(groups) for n in range(layers)]
    held = jnp.concatenate([weight_rows[pl.ds(pl.multiple_of(start, size), size), :] for start in starts], axis=0)
    fresh = (held.astype(f32) + step).astype(bf16)
    result = jnp.dot(left_side, fresh, preferred_element_type=f32).astype(bf16)
    activations[...] = result[: inputs.shape[0]]
    new_weight[...] = result[inputs.shape[0] : inputs.shape[0] + 1]


vmem = pl.BlockSpec(memory_space=pltpu.VMEM)
small_grant = pltpu.CompilerParams(vmem_limit_bytes=16 * 2**20)


def first_call(peers, momentum, gradient, basis, weight):
    arrays = [pltpu.with_memory_space_constraint(x, pltpu.HBM) for x in (momentum, gradient, basis, weight)]
    return pl.pallas_call(
        first_kernel,
        out_shape=jax.ShapeDtypeStruct((peers, 2, momentum.shape[1] + tail), bf16),
        in_specs=[pl.BlockSpec(memory_space=pltpu.HBM)] * 4,
        out_specs=vmem,
        scratch_shapes=[pltpu.VMEM(x.shape, x.dtype) for x in arrays] + [pltpu.SemaphoreType.DMA((4,))],
        compiler_params=small_grant,
        name="first",
    )(*arrays)


def second_call(peers, rank, upper_rows):
    rows = upper_rows.shape[0]
    return pl.pallas_call(
        second_kernel,
        out_shape=jax.ShapeDtypeStruct((peers, rows // 2 + rows // 4 + rank, rows), f32),
        in_specs=[vmem],
        out_specs=vmem,
        compiler_params=small_grant,
        name="second",
    )(upper_rows)


def third_call(scale, rank, near_size, place, layer, sums, upper_rows, weight_rows, momentum, gradient, inputs):
    width = weight_rows.shape[1]
    return pl.pallas_call(
        functools.partial(third_kernel, scale, near_size),
        out_shape=(
            jax.ShapeDtypeStruct((1, width), f32),
            jax.ShapeDtypeStruct((rank, width), f32),
            jax.ShapeDtypeStruct((1, width), bf16),
            jax.ShapeDtypeStruct((inputs.shape[0], width), bf16),
        ),
        in_specs=[pl.BlockSpec(memory_space=pltpu.SMEM)] * 2 + [vmem] * 6,
        out_specs=(vmem,) * 4,
        compiler_params=small_grant,
        name="third",
    )(place, layer, sums, upper_rows, weight_rows, momentum, gradient, inputs)


def on_device(momentum, gradient, basis, weight, inputs):
    zh, zl, a = (lax.axis_size(n) for n in rows_axes)
    rows = zh * zl * a
    width = momentum.shape[1]
    rank = basis.shape[0]
    peers = lax.axis_size("tp")
    scale = step_size * math.sqrt(width * peers / rows)
    far = spread(first_call(zh, momentum, gradient, basis, weight), "zh")
    upper_near = spread(replicated(far[:, 0], "zl"), "zl").reshape(zl * zh, width + tail)
    held = far[:, 1, :width]
    shifted = [lax.ppermute(held, "zl", [(i, (i + d) % zl) for i in range(zl)]) for d in range(1, zl)]
    upper_rows = lax.all_gather(upper_near, "a", axis=0, tiled=True)
    weight_rows = lax.all_gather(jnp.concatenate([held] + shifted, axis=0), "a", axis=0, tiled=True)
    sums = spread(second_call(peers, rank, upper_rows), "tp")
    place = (lax.axis_index("a") * zl + lax.axis_index("zl")) * zh + lax.axis_index("zh")
    ordered = inputs.reshape(-1, zh, zl, a).transpose(0, 3, 2, 1).reshape(-1, rows)
    place, layer = (x.reshape(1).astype(jnp.int32) for x in (place, lax.axis_index("zl")))
    return third_call(scale, rank, (a, zl, zh), place, layer, sums, upper_rows, weight_rows, momentum, gradient, ordered)


def solution(mesh):
    fsdp, tp = mesh.devices.shape
    fine = Mesh(mesh.devices.reshape(fsdp // 16, 4, 4, tp), rows_axes + ("tp",))
    return jax.shard_map(
        on_device,
        mesh=fine,
        in_specs=(
            P(rows_axes, "tp"),
            P(rows_axes, "tp"),
            P(None, "tp"),
            P(rows_axes, "tp"),
            P(rows_axes, None),
        ),
        out_specs=(P(rows_axes, "tp"), P(None, "tp"), P(rows_axes, "tp"), P(rows_axes, "tp")),
        check_vma=False,
    )
```

```python
import functools
import math

import jax
import jax.numpy as jnp
from jax import lax
from jax.experimental import pallas as pl
from jax.experimental.pallas import tpu as pltpu
from jax.sharding import Mesh, PartitionSpec as P


decay_rate = 0.8
step_size = 0.5
epsilon = 1e-06
highest = lax.Precision.HIGHEST
rows_axes = ("zh", "zl", "xl", "c")
tail = 128
bf16 = jnp.bfloat16
f32 = jnp.float32


def spread(blocks, axes):
    return lax.all_to_all(blocks, axes, 0, 0)


def replicated(block, axes):
    return jnp.broadcast_to(block[None], (lax.axis_size(axes),) + block.shape)


def iota(shape, dim):
    return lax.broadcasted_iota(jnp.int32, shape, dim)


def three_parts(x):
    high = x.astype(bf16).astype(f32)
    middle = (x - high).astype(bf16).astype(f32)
    return high, middle, x - high - middle


def inverse_root(x):
    guess = lax.rsqrt(x)
    return guess * (1.5 - 0.5 * x * guess * guess)


def first_kernel(momentum_hbm, gradient_hbm, basis_hbm, weight_hbm, out, momentum, gradient, basis, weight, arrived):
    pairs = ((momentum_hbm, momentum), (gradient_hbm, gradient), (basis_hbm, basis), (weight_hbm, weight))
    copies = [pltpu.make_async_copy(source, target, arrived.at[n]) for n, (source, target) in enumerate(pairs)]
    for copy in copies:
        copy.start()
    for copy in copies:
        copy.wait()
    width = momentum.shape[1]
    rank = basis.shape[0]
    total = jnp.zeros((rank, 128), f32)
    pieces = []
    for start in range(0, width, 128):
        cut = slice(start, start + 128)
        buffer = decay_rate * momentum[:, cut] + gradient[:, cut]
        pieces.append(buffer)
        total = total + basis[:, cut] * buffer
    sums = jnp.broadcast_to(jnp.sum(total, axis=1, keepdims=True), (rank, 128))
    lane, sub = iota((rank, 128), 1), iota((rank, 128), 0)
    row = jnp.sum(jnp.where(lane % rank == sub, sums, 0.0), axis=0, keepdims=True)
    high, middle, low = three_parts(row)
    place = iota((1, 128), 1)
    coded = jnp.where(place < rank, high, jnp.where(place < 2 * rank, middle, jnp.where(place < 3 * rank, low, 0.0)))
    upper = jnp.concatenate(pieces + [coded], axis=1).astype(bf16)
    under = jnp.concatenate([weight[...], jnp.zeros((1, tail), bf16)], axis=1)
    both = jnp.concatenate([upper, under], axis=0)
    for peer in range(out.shape[0]):
        out[peer] = both


def second_kernel(upper_rows, out):
    rows = upper_rows.shape[0]
    width = upper_rows.shape[1] - tail
    half, quarter = rows // 2, rows // 4
    rank = out.shape[1] - half - quarter
    buffer = upper_rows[:, :width]
    square = lax.dot_general(buffer, buffer, (((1,), (1,)), ((), ())), preferred_element_type=f32)
    corner = pltpu.roll(square[half + quarter :], quarter, 1)
    folded = jnp.where(iota((quarter, rows), 1) < quarter, corner, square[half : half + quarter])
    coded = upper_rows[:, width:].astype(f32).T
    power = coded[:rank] + coded[rank : 2 * rank] + coded[2 * rank : 3 * rank]
    for peer in range(out.shape[0]):
        out[peer, :half] = square[:half]
        out[peer, half : half + quarter] = folded
        out[peer, half + quarter :] = power


def quadratic(folded, vectors):
    rank, rows = vectors.shape
    half, quarter = rows // 2, rows // 4
    lane = iota((rank, rows), 1)
    in_third = (lane >= half) & (lane < half + quarter)
    turned = pltpu.roll(vectors, rows - quarter, 1)
    left = jnp.concatenate(
        [jnp.where(lane < half, vectors, 0.0), jnp.where(in_third, vectors, 0.0), jnp.where(in_third, turned, 0.0)], axis=0
    )
    right = jnp.concatenate([folded, jnp.zeros((quarter, rows), f32)], axis=0)
    along = lax.dot_general(left, right, (((1,), (0,)), ((), ())), precision=highest, preferred_element_type=f32)
    top = along[:rank] * vectors * jnp.where(lane < half, 1.0, 2.0)
    middle = along[rank : 2 * rank] * vectors * jnp.where(lane < half, 0.0, jnp.where(lane < half + quarter, 1.0, 2.0))
    corner = jnp.where(lane < quarter, along[2 * rank :] * pltpu.roll(vectors, quarter, 1), 0.0)
    return jnp.sum(top + middle + corner, axis=1, keepdims=True)


def third_kernel(
    scale, place, side, sums, upper_rows, weight_rows, momentum, gradient, inputs, new_momentum, new_basis, new_weight, activations
):
    rows, width = weight_rows.shape
    rank = new_basis.shape[0]
    total = sums[0]
    for peer in range(1, sums.shape[0]):
        total = total + sums[peer]
    folded, power = total[:-rank], total[-rank:]
    gram = lax.dot_general(power, power, (((1,), (1,)), ((), ())), precision=highest, preferred_element_type=f32)
    sub = iota((rank, rows), 0)
    columns = [jnp.broadcast_to(gram[:, k : k + 1], (rank, rows)) for k in range(rank)]
    ortho = power
    for k in range(rank):
        root = inverse_root(jnp.broadcast_to(columns[k][k : k + 1], (rank, rows)))
        factor = jnp.where(sub > k, columns[k] * root, 0.0)
        for j in range(k + 1, rank):
            columns[j] = columns[j] - factor * (columns[j][k : k + 1] * root[:1])
        ortho_row = ortho[k : k + 1] * root[:1]
        ortho = jnp.where(sub == k, ortho_row, ortho - factor * ortho_row)
    squares = jnp.maximum(quadratic(folded, ortho), 0.0)
    inverse = inverse_root(jnp.broadcast_to(squares, (rank, rows)) + epsilon)[:, :1]
    stacked = jnp.concatenate(three_parts(ortho), axis=0).astype(bf16)
    high, middle, low = three_parts(-scale * ortho)
    right_side = jnp.concatenate([high, high, middle, middle, high, low], axis=0)
    turned = jnp.concatenate([right_side, jnp.zeros((rows - 6 * rank, rows), f32)], axis=0).T.astype(bf16)
    here = place[0]
    own = jnp.sum(jnp.where(iota((rank, rows), 1) == here, ortho, 0.0), axis=1, keepdims=True) * (1.0 - decay_rate)
    chosen = (iota((16, rows), 1) == here).astype(f32).astype(bf16)
    left_side = jnp.concatenate([inputs[...], chosen], axis=0)
    parts = jnp.dot(stacked, upper_rows[:, :width], preferred_element_type=f32)
    coeff = parts[:rank] + parts[rank : 2 * rank] + parts[2 * rank :]
    buffer = decay_rate * momentum[...] + gradient[...]
    new_momentum[...] = buffer - jnp.sum(own * coeff, axis=0, keepdims=True)
    basis = coeff * inverse
    new_basis[...] = basis
    high, middle, low = three_parts(basis)
    under = jnp.concatenate([high, middle, high, middle, low, high], axis=0).astype(bf16)
    step = jnp.dot(turned[:, : 6 * rank], under, preferred_element_type=f32)
    block = rows // 4
    starts = [core * 2 * block + (at_x ^ side[0]) * block for at_x in range(2) for core in range(2)]
    held = jnp.concatenate([weight_rows[pl.ds(pl.multiple_of(start, block), block), :] for start in starts], axis=0)
    fresh = (held.astype(f32) + step).astype(bf16)
    result = jnp.dot(left_side, fresh, preferred_element_type=f32).astype(bf16)
    activations[...] = result[: inputs.shape[0]]
    new_weight[...] = result[inputs.shape[0] : inputs.shape[0] + 1]


vmem = pl.BlockSpec(memory_space=pltpu.VMEM)
small_grant = pltpu.CompilerParams(vmem_limit_bytes=16 * 2**20)


def first_call(peers, momentum, gradient, basis, weight):
    arrays = [pltpu.with_memory_space_constraint(x, pltpu.HBM) for x in (momentum, gradient, basis, weight)]
    return pl.pallas_call(
        first_kernel,
        out_shape=jax.ShapeDtypeStruct((peers, 2, momentum.shape[1] + tail), bf16),
        in_specs=[pl.BlockSpec(memory_space=pltpu.HBM)] * 4,
        out_specs=vmem,
        scratch_shapes=[pltpu.VMEM(x.shape, x.dtype) for x in arrays] + [pltpu.SemaphoreType.DMA((4,))],
        compiler_params=small_grant,
        name="first",
    )(*arrays)


def second_call(peers, rank, upper_rows):
    rows = upper_rows.shape[0]
    return pl.pallas_call(
        second_kernel,
        out_shape=jax.ShapeDtypeStruct((peers, rows // 2 + rows // 4 + rank, rows), f32),
        in_specs=[vmem],
        out_specs=vmem,
        compiler_params=small_grant,
        name="second",
    )(upper_rows)


def third_call(scale, rank, place, side, sums, upper_rows, weight_rows, momentum, gradient, inputs):
    width = weight_rows.shape[1]
    return pl.pallas_call(
        functools.partial(third_kernel, scale),
        out_shape=(
            jax.ShapeDtypeStruct((1, width), f32),
            jax.ShapeDtypeStruct((rank, width), f32),
            jax.ShapeDtypeStruct((1, width), bf16),
            jax.ShapeDtypeStruct((inputs.shape[0], width), bf16),
        ),
        in_specs=[pl.BlockSpec(memory_space=pltpu.SMEM)] * 2 + [vmem] * 6,
        out_specs=(vmem,) * 4,
        compiler_params=small_grant,
        name="third",
    )(place, side, sums, upper_rows, weight_rows, momentum, gradient, inputs)


def on_device(momentum, gradient, basis, weight, inputs):
    zh, zl, xl, c = (lax.axis_size(n) for n in rows_axes)
    rows = zh * zl * xl * c
    width = momentum.shape[1]
    rank = basis.shape[0]
    peers = lax.axis_size("tp")
    scale = step_size * math.sqrt(width * peers / rows)
    far = spread(first_call(zh, momentum, gradient, basis, weight), "zh")
    near = spread(replicated(far, "zl"), "zl").reshape(zl * zh, 2, width + tail)
    upper_rows = lax.all_gather(near[:, 0, :], ("xl", "c"), axis=0, tiled=True)
    weight_near = near[:, 1, :width]
    blocks = second_call(peers, rank, upper_rows)
    sums = spread(blocks, "tp")
    across = lax.ppermute(weight_near, "xl", [(0, 1), (1, 0)])
    weight_rows = lax.all_gather(jnp.concatenate([weight_near, across], axis=0), "c", axis=0, tiled=True)
    at_x = lax.axis_index("xl")
    place = ((at_x * c + lax.axis_index("c")) * zl + lax.axis_index("zl")) * zh + lax.axis_index("zh")
    ordered = inputs.reshape(-1, zh, zl, xl, c).transpose(0, 3, 4, 2, 1).reshape(-1, rows)
    place, side = (x.reshape(1).astype(jnp.int32) for x in (place, at_x))
    return third_call(scale, rank, place, side, sums, upper_rows, weight_rows, momentum, gradient, ordered)


def solution(mesh):
    fsdp, tp = mesh.devices.shape
    fine = Mesh(mesh.devices.reshape(fsdp // 16, 4, 2, 2, tp), rows_axes + ("tp",))
    return jax.shard_map(
        on_device,
        mesh=fine,
        in_specs=(
            P(rows_axes, "tp"),
            P(rows_axes, "tp"),
            P(None, "tp"),
            P(rows_axes, "tp"),
            P(rows_axes, None),
        ),
        out_specs=(P(rows_axes, "tp"), P(None, "tp"), P(rows_axes, "tp"), P(rows_axes, "tp")),
        check_vma=False,
    )
```

```python
import functools
import math

import jax
import jax.numpy as jnp
from jax import lax
from jax.experimental import pallas as pl
from jax.experimental.pallas import tpu as pltpu
from jax.sharding import Mesh, PartitionSpec as P

decay_rate = 0.8
step_size = 0.5
epsilon = 1e-06
highest = lax.Precision.HIGHEST
rows_axes = ("zh", "zl", "a")
tail = 128
bf16 = jnp.bfloat16
f32 = jnp.float32


def spread(blocks, axes):
    return lax.all_to_all(blocks, axes, 0, 0)


def replicated(block, axes):
    return jnp.broadcast_to(block[None], (lax.axis_size(axes),) + block.shape)


def iota(shape, dim):
    return lax.broadcasted_iota(jnp.int32, shape, dim)


def three_parts(x):
    high = x.astype(bf16).astype(f32)
    middle = (x - high).astype(bf16).astype(f32)
    return high, middle, x - high - middle


def inverse_root(x):
    guess = lax.rsqrt(x)
    return guess * (1.5 - 0.5 * x * guess * guess)


def first_kernel(momentum_hbm, gradient_hbm, basis_hbm, weight_hbm, out, momentum, gradient, basis, weight, arrived):
    pairs = ((momentum_hbm, momentum), (gradient_hbm, gradient), (basis_hbm, basis), (weight_hbm, weight))
    copies = [pltpu.make_async_copy(source, target, arrived.at[n]) for n, (source, target) in enumerate(pairs)]
    for copy in copies:
        copy.start()
    for copy in copies:
        copy.wait()
    width = momentum.shape[1]
    rank = basis.shape[0]
    total = jnp.zeros((rank, 128), f32)
    pieces = []
    for start in range(0, width, 128):
        cut = slice(start, start + 128)
        buffer = decay_rate * momentum[:, cut] + gradient[:, cut]
        pieces.append(buffer)
        total = total + basis[:, cut] * buffer
    sums = jnp.broadcast_to(jnp.sum(total, axis=1, keepdims=True), (rank, 128))
    lane, sub = iota((rank, 128), 1), iota((rank, 128), 0)
    row = jnp.sum(jnp.where(lane % rank == sub, sums, 0.0), axis=0, keepdims=True)
    high, middle, low = three_parts(row)
    place = iota((1, 128), 1)
    coded = jnp.where(place < rank, high, jnp.where(place < 2 * rank, middle, jnp.where(place < 3 * rank, low, 0.0)))
    upper = jnp.concatenate(pieces + [coded], axis=1).astype(bf16)
    under = jnp.concatenate([weight[...], jnp.zeros((1, tail), bf16)], axis=1)
    both = jnp.concatenate([upper, under], axis=0)
    for peer in range(out.shape[0]):
        out[peer] = both


def second_kernel(upper_rows, out):
    rows = upper_rows.shape[0]
    width = upper_rows.shape[1] - tail
    half, quarter, eighth = rows // 2, rows // 4, rows // 8
    rank = out.shape[1] - half - eighth
    buffer = upper_rows[:, :width]
    square = lax.dot_general(buffer, buffer, (((1,), (1,)), ((), ())), preferred_element_type=f32)
    corner = pltpu.roll(square[half + quarter :], quarter, 1)
    inner = jnp.where(iota((quarter, rows), 1) < quarter, corner, square[quarter:half])
    moved = pltpu.roll(square[half + eighth : half + quarter], half, 1)
    last = jnp.where(iota((eighth, rows), 1) < half, moved, square[half : half + eighth])
    coded = upper_rows[:, width:].astype(f32).T
    power = coded[:rank] + coded[rank : 2 * rank] + coded[2 * rank : 3 * rank]
    for peer in range(out.shape[0]):
        out[peer, :quarter] = square[:quarter]
        out[peer, quarter:half] = inner
        out[peer, half : half + eighth] = last
        out[peer, half + eighth :] = power


def quadratic(folded, vectors):
    rank, rows = vectors.shape
    half, quarter, eighth = rows // 2, rows // 4, rows // 8
    lane = iota((rank, rows), 1)

    def within(low, high, values):
        return jnp.where((lane >= low) & (lane < high), values, 0.0)

    def weights(start, single):
        return jnp.where(lane < start, 0.0, jnp.where(lane < single, 1.0, 2.0))

    by_quarter, by_half = pltpu.roll(vectors, quarter, 1), pltpu.roll(vectors, half, 1)
    left = jnp.concatenate(
        [
            within(0, quarter, vectors),
            within(quarter, half, vectors),
            within(quarter, half, by_half),
            within(half, half + eighth, vectors),
            within(half, half + eighth, pltpu.roll(vectors, rows - eighth, 1)),
        ],
        axis=0,
    )
    right = jnp.concatenate([folded, jnp.zeros((rows - half - eighth, rows), f32)], axis=0)
    along = lax.dot_general(left, right, (((1,), (0,)), ((), ())), precision=highest, preferred_element_type=f32)
    first, second, third, fourth, fifth = (along[n * rank : (n + 1) * rank] for n in range(5))
    plain = first * weights(0, quarter) + second * weights(quarter, half) + fourth * weights(half, half + quarter)
    total = plain * vectors + within(0, quarter, third) * by_quarter
    total = total + within(0, half, fifth * weights(0, quarter)) * by_half
    return jnp.sum(total, axis=1, keepdims=True)


def third_kernel(
    scale, place, sums, upper_rows, weight_rows, momentum, gradient, inputs, new_momentum, new_basis, new_weight, activations
):
    rows, width = weight_rows.shape
    rank = new_basis.shape[0]
    total = sums[0]
    for peer in range(1, sums.shape[0]):
        total = total + sums[peer]
    folded, power = total[:-rank], total[-rank:]
    gram = lax.dot_general(power, power, (((1,), (1,)), ((), ())), precision=highest, preferred_element_type=f32)
    sub = iota((rank, rows), 0)
    columns = [jnp.broadcast_to(gram[:, k : k + 1], (rank, rows)) for k in range(rank)]
    ortho = power
    for k in range(rank):
        root = inverse_root(jnp.broadcast_to(columns[k][k : k + 1], (rank, rows)))
        factor = jnp.where(sub > k, columns[k] * root, 0.0)
        for j in range(k + 1, rank):
            columns[j] = columns[j] - factor * (columns[j][k : k + 1] * root[:1])
        ortho_row = ortho[k : k + 1] * root[:1]
        ortho = jnp.where(sub == k, ortho_row, ortho - factor * ortho_row)
    squares = jnp.maximum(quadratic(folded, ortho), 0.0)
    inverse = inverse_root(jnp.broadcast_to(squares, (rank, rows)) + epsilon)[:, :1]
    stacked = jnp.concatenate(three_parts(ortho), axis=0).astype(bf16)
    high, middle, low = three_parts(-scale * ortho)
    right_side = jnp.concatenate([high, high, middle, middle, high, low], axis=0)
    turned = jnp.concatenate([right_side, jnp.zeros((rows - 6 * rank, rows), f32)], axis=0).T.astype(bf16)
    here = place[0]
    own = jnp.sum(jnp.where(iota((rank, rows), 1) == here, ortho, 0.0), axis=1, keepdims=True) * (1.0 - decay_rate)
    chosen = (iota((16, rows), 1) == here).astype(f32).astype(bf16)
    left_side = jnp.concatenate([inputs[...], chosen], axis=0)
    parts = jnp.dot(stacked, upper_rows[:, :width], preferred_element_type=f32)
    coeff = parts[:rank] + parts[rank : 2 * rank] + parts[2 * rank :]
    buffer = decay_rate * momentum[...] + gradient[...]
    new_momentum[...] = buffer - jnp.sum(own * coeff, axis=0, keepdims=True)
    basis = coeff * inverse
    new_basis[...] = basis
    high, middle, low = three_parts(basis)
    under = jnp.concatenate([high, middle, high, middle, low, high], axis=0).astype(bf16)
    step = jnp.dot(turned[:, : 6 * rank], under, preferred_element_type=f32)
    fresh = (weight_rows[...].astype(f32) + step).astype(bf16)
    result = jnp.dot(left_side, fresh, preferred_element_type=f32).astype(bf16)
    activations[...] = result[: inputs.shape[0]]
    new_weight[...] = result[inputs.shape[0] : inputs.shape[0] + 1]


vmem = pl.BlockSpec(memory_space=pltpu.VMEM)
small_grant = pltpu.CompilerParams(vmem_limit_bytes=16 * 2**20)


def first_call(peers, momentum, gradient, basis, weight):
    arrays = [pltpu.with_memory_space_constraint(x, pltpu.HBM) for x in (momentum, gradient, basis, weight)]
    return pl.pallas_call(
        first_kernel,
        out_shape=jax.ShapeDtypeStruct((peers, 2, momentum.shape[1] + tail), bf16),
        in_specs=[pl.BlockSpec(memory_space=pltpu.HBM)] * 4,
        out_specs=vmem,
        scratch_shapes=[pltpu.VMEM(x.shape, x.dtype) for x in arrays] + [pltpu.SemaphoreType.DMA((4,))],
        compiler_params=small_grant,
        name="first",
    )(*arrays)


def second_call(peers, rank, upper_rows):
    rows = upper_rows.shape[0]
    return pl.pallas_call(
        second_kernel,
        out_shape=jax.ShapeDtypeStruct((peers, rows // 2 + rows // 8 + rank, rows), f32),
        in_specs=[vmem],
        out_specs=vmem,
        compiler_params=small_grant,
        name="second",
    )(upper_rows)


def third_call(scale, rank, place, sums, upper_rows, weight_rows, momentum, gradient, inputs):
    width = weight_rows.shape[1]
    return pl.pallas_call(
        functools.partial(third_kernel, scale),
        out_shape=(
            jax.ShapeDtypeStruct((1, width), f32),
            jax.ShapeDtypeStruct((rank, width), f32),
            jax.ShapeDtypeStruct((1, width), bf16),
            jax.ShapeDtypeStruct((inputs.shape[0], width), bf16),
        ),
        in_specs=[pl.BlockSpec(memory_space=pltpu.SMEM)] + [vmem] * 6,
        out_specs=(vmem,) * 4,
        compiler_params=small_grant,
        name="third",
    )(place, sums, upper_rows, weight_rows, momentum, gradient, inputs)


def on_device(momentum, gradient, basis, weight, inputs):
    zh, zl, a = (lax.axis_size(n) for n in rows_axes)
    rows = zh * zl * a
    width = momentum.shape[1]
    rank = basis.shape[0]
    peers = lax.axis_size("tp")
    scale = step_size * math.sqrt(width * peers / rows)
    far = spread(first_call(zh, momentum, gradient, basis, weight), "zh")
    near = spread(replicated(far, "zl"), "zl").reshape(zl * zh, 2, width + tail)
    upper_rows = lax.all_gather(near[:, 0, :], "a", axis=0, tiled=True)
    weight_rows = lax.all_gather(near[:, 1, :width], "a", axis=0, tiled=True)
    sums = spread(second_call(peers, rank, upper_rows), "tp")
    place = (lax.axis_index("a") * zl + lax.axis_index("zl")) * zh + lax.axis_index("zh")
    ordered = inputs.reshape(-1, zh, zl, a).transpose(0, 3, 2, 1).reshape(-1, rows)
    return third_call(
        scale, rank, place.reshape(1).astype(jnp.int32), sums, upper_rows, weight_rows, momentum, gradient, ordered
    )


def solution(mesh):
    fsdp, tp = mesh.devices.shape
    fine = Mesh(mesh.devices.reshape(fsdp // 16, 4, 4, tp), rows_axes + ("tp",))
    return jax.shard_map(
        on_device,
        mesh=fine,
        in_specs=(
            P(rows_axes, "tp"),
            P(rows_axes, "tp"),
            P(None, "tp"),
            P(rows_axes, "tp"),
            P(rows_axes, None),
        ),
        out_specs=(P(rows_axes, "tp"), P(None, "tp"), P(rows_axes, "tp"), P(rows_axes, "tp")),
        check_vma=False,
    )
```

```python
import functools
import math

import jax
import jax.numpy as jnp
from jax import lax
from jax.experimental import pallas as pl
from jax.experimental.pallas import tpu as pltpu
from jax.sharding import Mesh, PartitionSpec as P

decay_rate = 0.8
step_size = 0.5
epsilon = 1e-06
highest = lax.Precision.HIGHEST
rows_axes = ("zh", "zl", "a")
tail = 128
bf16 = jnp.bfloat16
f32 = jnp.float32


def spread(blocks, axes):
    return lax.all_to_all(blocks, axes, 0, 0)


def replicated(block, axes):
    return jnp.broadcast_to(block[None], (lax.axis_size(axes),) + block.shape)


def iota(shape, dim):
    return lax.broadcasted_iota(jnp.int32, shape, dim)


def three_parts(x):
    high = x.astype(bf16).astype(f32)
    middle = (x - high).astype(bf16).astype(f32)
    return high, middle, x - high - middle


def inverse_root(x):
    guess = lax.rsqrt(x)
    return guess * (1.5 - 0.5 * x * guess * guess)


def first_kernel(momentum_hbm, gradient_hbm, basis_hbm, weight_hbm, out, momentum, gradient, basis, weight, arrived):
    pairs = ((momentum_hbm, momentum), (gradient_hbm, gradient), (basis_hbm, basis), (weight_hbm, weight))
    copies = [pltpu.make_async_copy(source, target, arrived.at[n]) for n, (source, target) in enumerate(pairs)]
    for copy in copies:
        copy.start()
    for copy in copies:
        copy.wait()
    width = momentum.shape[1]
    rank = basis.shape[0]
    total = jnp.zeros((rank, 128), f32)
    pieces = []
    for start in range(0, width, 128):
        cut = slice(start, start + 128)
        buffer = decay_rate * momentum[:, cut] + gradient[:, cut]
        pieces.append(buffer)
        total = total + basis[:, cut] * buffer
    sums = jnp.broadcast_to(jnp.sum(total, axis=1, keepdims=True), (rank, 128))
    lane, sub = iota((rank, 128), 1), iota((rank, 128), 0)
    row = jnp.sum(jnp.where(lane % rank == sub, sums, 0.0), axis=0, keepdims=True)
    high, middle, low = three_parts(row)
    place = iota((1, 128), 1)
    coded = jnp.where(place < rank, high, jnp.where(place < 2 * rank, middle, jnp.where(place < 3 * rank, low, 0.0)))
    upper = jnp.concatenate(pieces + [coded], axis=1).astype(bf16)
    under = jnp.concatenate([weight[...], jnp.zeros((1, tail), bf16)], axis=1)
    both = jnp.concatenate([upper, under], axis=0)
    for peer in range(out.shape[0]):
        out[peer] = both


def second_kernel(upper_rows, out):
    rows = upper_rows.shape[0]
    width = upper_rows.shape[1] - tail
    half, quarter, eighth = rows // 2, rows // 4, rows // 8
    rank = out.shape[1] - half - eighth
    buffer = upper_rows[:, :width]
    square = lax.dot_general(buffer, buffer, (((1,), (1,)), ((), ())), preferred_element_type=f32)
    corner = pltpu.roll(square[half + quarter :], quarter, 1)
    inner = jnp.where(iota((quarter, rows), 1) < quarter, corner, square[quarter:half])
    moved = pltpu.roll(square[half + eighth : half + quarter], half, 1)
    last = jnp.where(iota((eighth, rows), 1) < half, moved, square[half : half + eighth])
    coded = upper_rows[:, width:].astype(f32).T
    power = coded[:rank] + coded[rank : 2 * rank] + coded[2 * rank : 3 * rank]
    for peer in range(out.shape[0]):
        out[peer, :quarter] = square[:quarter]
        out[peer, quarter:half] = inner
        out[peer, half : half + eighth] = last
        out[peer, half + eighth :] = power


def quadratic(folded, vectors):
    rank, rows = vectors.shape
    half, quarter, eighth = rows // 2, rows // 4, rows // 8
    lane = iota((rank, rows), 1)

    def within(low, high, values):
        return jnp.where((lane >= low) & (lane < high), values, 0.0)

    def weights(start, single):
        return jnp.where(lane < start, 0.0, jnp.where(lane < single, 1.0, 2.0))

    by_quarter, by_half = pltpu.roll(vectors, quarter, 1), pltpu.roll(vectors, half, 1)
    left = jnp.concatenate(
        [
            within(0, quarter, vectors),
            within(quarter, half, vectors),
            within(quarter, half, by_half),
            within(half, half + eighth, vectors),
            within(half, half + eighth, pltpu.roll(vectors, rows - eighth, 1)),
        ],
        axis=0,
    )
    right = jnp.concatenate([folded, jnp.zeros((rows - half - eighth, rows), f32)], axis=0)
    along = lax.dot_general(left, right, (((1,), (0,)), ((), ())), precision=highest, preferred_element_type=f32)
    first, second, third, fourth, fifth = (along[n * rank : (n + 1) * rank] for n in range(5))
    plain = first * weights(0, quarter) + second * weights(quarter, half) + fourth * weights(half, half + quarter)
    total = plain * vectors + within(0, quarter, third) * by_quarter
    total = total + within(0, half, fifth * weights(0, quarter)) * by_half
    return jnp.sum(total, axis=1, keepdims=True)


def third_kernel(
    scale, sums, upper_rows, weight_rows, momentum, gradient, inputs, new_momentum, new_basis, new_weight, activations
):
    rows, width = weight_rows.shape
    rank = new_basis.shape[0]
    total = sums[0]
    for peer in range(1, sums.shape[0]):
        total = total + sums[peer]
    folded, power = total[:-rank], total[-rank:]
    gram = lax.dot_general(power, power, (((1,), (1,)), ((), ())), precision=highest, preferred_element_type=f32)
    sub = iota((rank, rows), 0)
    columns = [jnp.broadcast_to(gram[:, k : k + 1], (rank, rows)) for k in range(rank)]
    ortho = power
    for k in range(rank):
        root = inverse_root(jnp.broadcast_to(columns[k][k : k + 1], (rank, rows)))
        factor = jnp.where(sub > k, columns[k] * root, 0.0)
        for j in range(k + 1, rank):
            columns[j] = columns[j] - factor * (columns[j][k : k + 1] * root[:1])
        ortho_row = ortho[k : k + 1] * root[:1]
        ortho = jnp.where(sub == k, ortho_row, ortho - factor * ortho_row)
    squares = jnp.maximum(quadratic(folded, ortho), 0.0)
    inverse = inverse_root(jnp.broadcast_to(squares, (rank, rows)) + epsilon)[:, :1]
    stacked = jnp.concatenate(three_parts(ortho), axis=0).astype(bf16)
    high, middle, low = three_parts(-scale * ortho)
    right_side = jnp.concatenate([high, high, middle, middle, high, low], axis=0)
    turned = jnp.concatenate([right_side, jnp.zeros((rows - 6 * rank, rows), f32)], axis=0).T.astype(bf16)
    zh, zl = lax.axis_size("zh"), lax.axis_size("zl")
    here = (lax.axis_index("a") * zl + lax.axis_index("zl")) * zh + lax.axis_index("zh")
    own = jnp.sum(jnp.where(iota((rank, rows), 1) == here, ortho, 0.0), axis=1, keepdims=True) * (1.0 - decay_rate)
    chosen = (iota((16, rows), 1) == here).astype(f32).astype(bf16)
    left_side = jnp.concatenate([inputs[...], chosen], axis=0)
    parts = jnp.dot(stacked, upper_rows[:, :width], preferred_element_type=f32)
    coeff = parts[:rank] + parts[rank : 2 * rank] + parts[2 * rank :]
    buffer = decay_rate * momentum[...] + gradient[...]
    new_momentum[...] = buffer - jnp.sum(own * coeff, axis=0, keepdims=True)
    basis = coeff * inverse
    new_basis[...] = basis
    high, middle, low = three_parts(basis)
    under = jnp.concatenate([high, middle, high, middle, low, high], axis=0).astype(bf16)
    step = jnp.dot(turned[:, : 6 * rank], under, preferred_element_type=f32)
    fresh = (weight_rows[...].astype(f32) + step).astype(bf16)
    result = jnp.dot(left_side, fresh, preferred_element_type=f32).astype(bf16)
    activations[...] = result[: inputs.shape[0]]
    new_weight[...] = result[inputs.shape[0] : inputs.shape[0] + 1]


vmem = pl.BlockSpec(memory_space=pltpu.VMEM)
small_grant = pltpu.CompilerParams(vmem_limit_bytes=16 * 2**20)


def first_call(peers, momentum, gradient, basis, weight):
    arrays = [pltpu.with_memory_space_constraint(x, pltpu.HBM) for x in (momentum, gradient, basis, weight)]
    return pl.pallas_call(
        first_kernel,
        out_shape=jax.ShapeDtypeStruct((peers, 2, momentum.shape[1] + tail), bf16),
        in_specs=[pl.BlockSpec(memory_space=pltpu.HBM)] * 4,
        out_specs=vmem,
        scratch_shapes=[pltpu.VMEM(x.shape, x.dtype) for x in arrays] + [pltpu.SemaphoreType.DMA((4,))],
        compiler_params=small_grant,
        name="first",
    )(*arrays)


def second_call(peers, rank, upper_rows):
    rows = upper_rows.shape[0]
    return pl.pallas_call(
        second_kernel,
        out_shape=jax.ShapeDtypeStruct((peers, rows // 2 + rows // 8 + rank, rows), f32),
        in_specs=[vmem],
        out_specs=vmem,
        compiler_params=small_grant,
        name="second",
    )(upper_rows)


def third_call(scale, rank, sums, upper_rows, weight_rows, momentum, gradient, inputs):
    width = weight_rows.shape[1]
    return pl.pallas_call(
        functools.partial(third_kernel, scale),
        out_shape=(
            jax.ShapeDtypeStruct((1, width), f32),
            jax.ShapeDtypeStruct((rank, width), f32),
            jax.ShapeDtypeStruct((1, width), bf16),
            jax.ShapeDtypeStruct((inputs.shape[0], width), bf16),
        ),
        in_specs=[vmem] * 6,
        out_specs=(vmem,) * 4,
        compiler_params=small_grant,
        name="third",
    )(sums, upper_rows, weight_rows, momentum, gradient, inputs)


def on_device(momentum, gradient, basis, weight, inputs):
    zh, zl, a = (lax.axis_size(n) for n in rows_axes)
    rows = zh * zl * a
    width = momentum.shape[1]
    rank = basis.shape[0]
    peers = lax.axis_size("tp")
    scale = step_size * math.sqrt(width * peers / rows)
    far = spread(first_call(zh, momentum, gradient, basis, weight), "zh")
    near = spread(replicated(far, "zl"), "zl").reshape(zl * zh, 2, width + tail)
    upper_rows = lax.all_gather(near[:, 0, :], "a", axis=0, tiled=True)
    weight_rows = lax.all_gather(near[:, 1, :width], "a", axis=0, tiled=True)
    inputs, blocks = lax.optimization_barrier((inputs, second_call(peers, rank, upper_rows)))
    sums = spread(blocks, "tp")
    ordered = inputs.reshape(-1, zh, zl, a).transpose(0, 3, 2, 1).reshape(-1, rows)
    return third_call(scale, rank, sums, upper_rows, weight_rows, momentum, gradient, ordered)


def solution(mesh):
    fsdp, tp = mesh.devices.shape
    fine = Mesh(mesh.devices.reshape(fsdp // 16, 4, 4, tp), rows_axes + ("tp",))
    return jax.shard_map(
        on_device,
        mesh=fine,
        in_specs=(
            P(rows_axes, "tp"),
            P(rows_axes, "tp"),
            P(None, "tp"),
            P(rows_axes, "tp"),
            P(rows_axes, None),
        ),
        out_specs=(P(rows_axes, "tp"), P(None, "tp"), P(rows_axes, "tp"), P(rows_axes, "tp")),
        check_vma=False,
    )
```
